256 devices in a mesh: dp: 16 (over x, y_lo, core), fsdp: 16 (over z, y_hi).
Axes of the slice: x: 4, y: 4 (y_hi: 2, y_lo: 2; y = y_hi * 2 + y_lo), z: 8, core: 2. Of those that a mesh axis runs over, the one named last changes fastest.
Arguments:
- fields: bfloat16 [16, 6, 48, 48, 48, 128], P('dp', None, 'fsdp'), may hold values from -6 to 6
- targets: bfloat16 [16, 6, 48, 2304], P('dp', None, 'fsdp'), may hold values from -6 to 6
- lists: int32 [16, 6], P('dp'), may hold values from 0 to 5, each once within a row
- counts: int32 [16], replicated, may hold values from 1 to 6, as said below
- spectral_w: bfloat16 [32, 2, 128, 128], P('fsdp'), may hold values from -0.375 to 0.375
- local_w: bfloat16 [128, 128], replicated, may hold values from -0.5 to 0.5
- proj: float32 [128], replicated, may hold values from -0.5 to 0.5
Outputs:
- grad_spectral: float32 [32, 2, 128, 128], P('fsdp')
- grad_local: float32 [128, 128], replicated
The draws below stay inside these ranges and needn't reach their ends.
Inputs may be any that keep to these rules, and one draw needn't show every extreme that they name: Each row of lists names every slot of its lane once; the first counts[l] entries of row l are lane l's live grids. `counts`: exactly one lane has 6 live grids; every other lane has 1 or 2.
All inputs are finite; a program needn't handle non-finite values.
Results may differ from the reference program's by a relative error of at most 0.0036.
The reference program's roundings to bfloat16 on the way count: a program that leaves them out, or rounds other values in their place, can miss the bound.
Values may be sent and summed in bfloat16 or wider, within the bound.
A program may use at most 64 MiB of HBM per device.

```python
import math
import jax
import jax.numpy as jnp
from jax import lax

C = 128
G = 48
MX = 4
MY = 4
MZ = 2
MODES = 32
SLOTS = 6
N_DP = 16


def draw_counts(key, part):
    base_counts = jax.random.randint(jax.random.fold_in(key, 11), (N_DP,), 1, 3, dtype=jnp.int32)
    busiest = jax.random.randint(jax.random.fold_in(key, 12), (), 0, N_DP, dtype=jnp.int32)
    return jnp.where(jnp.arange(N_DP, dtype=jnp.int32) == busiest, SLOTS, base_counts).astype(jnp.int32)


def steps_of(stream_key, shape, pieces, smallest, high):
    loudness = 1.0
    for dim, parts in pieces:
        steps = jax.random.uniform(jax.random.fold_in(jax.random.fold_in(stream_key, 6), dim), (parts,), jnp.float32, smallest / len(pieces), high / len(pieces))
        loudness = loudness * jnp.repeat(jnp.exp(steps), shape[dim] // parts).reshape((-1,) + (1,) * (len(shape) - 1 - dim))
    return loudness


def scatter_about(rng, shape, scale, reach, cuts=(), kind=jnp.bfloat16):
    values = scale * jax.random.normal(rng, shape, jnp.float32)
    if cuts:
        values = values * steps_of(rng, shape, cuts, -0.22, 0.18)
    return jnp.clip(values, -reach, reach).astype(kind)


def setup_inputs(seed: int = 0) -> dict:
    seeds = jax.random.split(jax.random.key(seed), 8)
    fields = scatter_about(seeds[0], (N_DP, SLOTS, G, G, G, C), 1.0, 6.0, ((0, 16), (2, 16)))
    targets = scatter_about(seeds[1], (N_DP, SLOTS, G, G * G), 1.0, 6.0, ((0, 16), (2, 16)))
    lists = jax.vmap(lambda own: jax.random.permutation(own, SLOTS))(jax.random.split(seeds[2], N_DP)).reshape((N_DP, SLOTS)).astype(jnp.int32)
    counts = draw_counts(jax.random.fold_in(seeds[7], 71), 0)
    spectral_w = scatter_about(seeds[4], (MODES, 2, C, C), (2 * C) ** -0.5, 0.375, ((0, 16),))
    local_w = scatter_about(seeds[5], (C, C), C ** -0.5, 0.5)
    proj = scatter_about(seeds[6], (C,), C ** -0.5, 0.5, (), jnp.float32)
    return dict(fields=fields, targets=targets, lists=lists, counts=counts, spectral_w=spectral_w, local_w=local_w, proj=proj)


highest = lax.Precision.HIGHEST
root_half = 0.7071067811865476
inv_root_two_pi = 0.3989422804014327

def phase_table(mode_ids, cell_ids, length, direction):
    product = mode_ids[:, None] * cell_ids[None, :] % length
    angle = product.astype(jnp.float32) * (2.0 * math.pi / length)
    return (jnp.cos(angle), direction * jnp.sin(angle))

def mode_lists():
    kx_ids = jnp.arange(MX, dtype=jnp.int32) - MX // 2
    ky_ids = jnp.arange(MY, dtype=jnp.int32) - MY // 2
    kz_ids = jnp.arange(MZ, dtype=jnp.int32)
    return (kx_ids, ky_ids, kz_ids)

def complex_contract(real_part, imag_part, cos_t, sin_t, form):

    def product(left, right):
        return jnp.einsum(form, left, right, precision=highest)
    return (product(real_part, cos_t) - product(imag_part, sin_t), product(real_part, sin_t) + product(imag_part, cos_t))

def forward_modes(grid_field, x_cells, scale):
    grid_len = grid_field.shape[1]
    kx_ids, ky_ids, kz_ids = mode_lists()
    cells = jnp.arange(grid_len, dtype=jnp.int32)
    cos_z, sin_z = phase_table(kz_ids, cells, grid_len, -1.0)
    cos_zb = lax.optimization_barrier(cos_z.astype(jnp.bfloat16)).astype(jnp.float32)
    sin_zb = lax.optimization_barrier(sin_z.astype(jnp.bfloat16)).astype(jnp.float32)
    field_wide = grid_field.astype(jnp.float32)
    part_re = jnp.einsum('abzc,kz->abkc', field_wide, cos_zb, precision=highest)
    part_im = jnp.einsum('abzc,kz->abkc', field_wide, sin_zb, precision=highest)
    cos_y, sin_y = phase_table(ky_ids, cells, grid_len, -1.0)
    next_re, next_im = complex_contract(part_re, part_im, cos_y, sin_y, 'abkc,jb->ajkc')
    cos_x, sin_x = phase_table(kx_ids, x_cells, grid_len, -1.0)
    last_re, last_im = complex_contract(next_re, next_im, cos_x, sin_x, 'ajkc,ia->ijkc')
    stacked = jnp.stack([last_re, last_im], axis=3) * scale
    return stacked.reshape(MX * MY * MZ, 2, stacked.shape[-1])

def inverse_modes(spectrum, x_cells, grid_len):
    kx_ids, ky_ids, kz_ids = mode_lists()
    cells = jnp.arange(grid_len, dtype=jnp.int32)
    values = spectrum.astype(jnp.float32).reshape(MX, MY, MZ, 2, spectrum.shape[-1])
    cos_x, sin_x = phase_table(kx_ids, x_cells, grid_len, 1.0)
    first_re, first_im = complex_contract(values[:, :, :, 0], values[:, :, :, 1], cos_x, sin_x, 'ijkc,ia->ajkc')
    cos_y, sin_y = phase_table(ky_ids, cells, grid_len, 1.0)
    second_re, second_im = complex_contract(first_re, first_im, cos_y, sin_y, 'ajkc,jb->abkc')
    cos_z, sin_z = phase_table(kz_ids, cells, grid_len, 1.0)
    real_out = jnp.einsum('abkc,kz->abzc', second_re, cos_z, precision=highest)
    real_out = real_out - jnp.einsum('abkc,kz->abzc', second_im, sin_z, precision=highest)
    return real_out * float(MX * MY * MZ) ** (-0.5)

def mix_modes(coeff_b, weights):
    coeff_f = coeff_b.astype(jnp.float32)
    weight_f = weights.astype(jnp.float32)
    signs = jnp.array([1.0, -1.0], jnp.float32).reshape(1, 2, 1, 1)
    spec_re = jnp.einsum('gmri,mrio->gmo', coeff_f, weight_f * signs, precision=highest)
    spec_im = jnp.einsum('gmri,mrio->gmo', coeff_f[:, :, ::-1], weight_f, precision=highest)
    return jnp.stack([spec_re, spec_im], axis=2)

def weight_grad(coeff_b, back_stack):
    coeff_f = coeff_b.astype(jnp.float32)
    rotated = jnp.stack([-coeff_f[:, :, 1], coeff_f[:, :, 0]], axis=2)
    grad_re = jnp.einsum('gmri,gmro->mio', coeff_f, back_stack, precision=highest)
    grad_im = jnp.einsum('gmri,gmro->mio', rotated, back_stack, precision=highest)
    return jnp.stack([grad_re, grad_im], axis=1)

def point_part(grid_field, branch, local_w, proj, grid_target, scale):
    width = grid_field.shape[-1]
    flat_field = grid_field.reshape(-1, width)
    pre = branch.reshape(-1, width) + jnp.dot(flat_field, local_w, preferred_element_type=jnp.float32)
    erf_part = lax.erf(pre * root_half)
    active = 0.5 * pre * (1.0 + erf_part)
    pred = jnp.dot(active, proj, precision=highest)
    resid = (pred - grid_target.reshape(-1).astype(jnp.float32)) * scale
    slope = 0.5 * (1.0 + erf_part) + pre * jnp.exp(-0.5 * pre * pre) * inv_root_two_pi
    d_pre = (resid[:, None] * proj[None, :] * slope).astype(jnp.bfloat16)
    local_grad = jnp.dot(flat_field.T, d_pre, preferred_element_type=jnp.float32)
    return (d_pre.reshape(grid_field.shape), local_grad)

def reference(fields, targets, lists, counts, spectral_w, local_w, proj):
    slot_ids = jnp.arange(SLOTS, dtype=jnp.int32)
    lane_ids = jnp.arange(N_DP, dtype=jnp.int32)
    keyed = jnp.where(slot_ids[None, :] < counts[:, None], lane_ids[:, None] * SLOTS + lists, N_DP * SLOTS)
    ordered = jnp.sort(keyed.reshape(-1)).astype(jnp.int32)
    grid_total = jnp.sum(counts).astype(jnp.int32)
    scale = 1.0 / grid_total.astype(jnp.float32)
    all_fields = fields.reshape(N_DP * SLOTS, G, G, G, C)
    all_targets = targets.reshape(N_DP * SLOTS, G, G * G)
    x_cells = jnp.arange(G, dtype=jnp.int32)
    mode_scale = float(MODES) ** (-0.5)

    def visit(position, carry):
        grad_spectral, grad_local = carry
        which = ordered[position].astype(jnp.int32)
        grid_field = lax.dynamic_index_in_dim(all_fields, which, 0, keepdims=False)
        grid_target = lax.dynamic_index_in_dim(all_targets, which, 0, keepdims=False)
        coeff_b = forward_modes(grid_field, x_cells, float(G) ** (-1.5)).astype(jnp.bfloat16)
        spectrum = mix_modes(coeff_b[None], spectral_w)[0].astype(jnp.bfloat16)
        branch = inverse_modes(spectrum, x_cells, G)
        d_pre, local_grad = point_part(grid_field, branch, local_w, proj, grid_target, scale)
        grid_back = forward_modes(d_pre, x_cells, mode_scale)
        return (grad_spectral + weight_grad(coeff_b[None], grid_back[None]), grad_local + local_grad)
    start = (jnp.zeros((MODES, 2, C, C), jnp.float32), jnp.zeros((C, C), jnp.float32))
    grad_spectral, grad_local = lax.fori_loop(0, grid_total, visit, start)
    return (grad_spectral, grad_local)
```

```python
import functools
import math

import jax
import jax.numpy as jnp
import numpy as np
from jax import lax
from jax.experimental import pallas as pl
from jax.experimental.pallas import tpu as pltpu
from jax.sharding import PartitionSpec as P

MX, MY, MZ = 4, 4, 2
N_DEV = 16
ROWS = MY * MZ * 2
ROOT_HALF = 0.7071067811865476
INV_ROOT_TWO_PI = 0.3989422804014327
LOG2_E = 1.4426950408889634
MESH = pl.DeviceIdType.MESH
CHUNK = 768


def phases(ids, length):
    product = (ids[:, None] * np.arange(length)[None, :]) % length
    angle = product.astype(np.float32) * np.float32(2.0 * math.pi / length)
    return np.cos(angle).astype(np.float32), np.sin(angle).astype(np.float32)


def split_bf16(values):
    high = values.astype(jnp.bfloat16)
    low = (values - high.astype(np.float32)).astype(jnp.bfloat16)
    return high, low


@functools.lru_cache(maxsize=None)
def tables(length):
    cos_x, sin_x = phases(np.arange(MX) - MX // 2, length)
    cos_y, sin_y = phases(np.arange(MY) - MY // 2, length)
    cos_z, sin_z = phases(np.arange(MZ), length)
    round_z = lambda t: t.astype(jnp.bfloat16).astype(np.float32)

    def product(cz, sz):
        re = cos_y[:, None, :, None] * cz[None, :, None, :] - sin_y[:, None, :, None] * sz[None, :, None, :]
        im = sin_y[:, None, :, None] * cz[None, :, None, :] + cos_y[:, None, :, None] * sz[None, :, None, :]
        shape = (MY, MZ, length * length)
        return re.reshape(shape), -im.reshape(shape)

    re, im = product(round_z(cos_z), round_z(sin_z))
    direct = np.stack([re, im], axis=2).reshape(ROWS, -1)
    turned = np.stack([im, -re], axis=2).reshape(ROWS, -1)
    forward = np.concatenate([*split_bf16(direct), *split_bf16(turned)], axis=0)
    re, im = product(cos_z, sin_z)
    back = np.stack([re, im], axis=2).reshape(ROWS, -1).T * np.float32(float(MX * MY * MZ) ** -0.5)
    high, low = split_bf16(back)
    inverse = np.concatenate([high, low, high], axis=1)
    return np.stack([cos_x, sin_x]).reshape(2, -1), forward, inverse


def times_i(values):
    rows, width = values.shape
    grouped = values.reshape(rows // 8, 8, width)
    even = lax.broadcasted_iota(jnp.int32, grouped.shape, 1) % 2 == 0
    turned = jnp.where(even, -pltpu.roll(grouped, 7, 1), pltpu.roll(grouped, 1, 1))
    return turned.reshape(rows, width)


def dot(a, b):
    return jnp.dot(a, b, preferred_element_type=jnp.float32)


def dot_t(a, b):
    return lax.dot_general(a, b, (((0,), (0,)), ((), ())), preferred_element_type=jnp.float32)


def kernel(
    length, slots, planes,
    fields, cell_table, fwd_table, spec_w, local_w, proj, lists, counts, xphase,
    out_spec, out_local,
    fbuf, rhs, inv_rows, acc, local_acc,
    c_send, c_recv, s_send, s_recv, cg_send, cg_recv, b_send, b_recv, bg_send, bg_recv,
    l_send, l_recv, m_send, m_recv, n_send, n_recv,
    load_sem, send_sem, recv_sem,
):
    cells = length * length
    width = fields.shape[-1]
    rows = slots * 4
    me = {"fsdp": lax.axis_index("fsdp"), "dp": lax.axis_index("dp")}

    def peer_of(axis, t):
        offset = 8 + ((t + 1) // 2) * (1 - 2 * (t % 2))
        return lax.rem(me[axis] + offset, N_DEV)

    def start_exchange(phase, axis, src, dst):
        def one(t, carry):
            peer = peer_of(axis, t)
            pltpu.make_async_remote_copy(
                src_ref=src(peer), dst_ref=dst(me[axis]),
                send_sem=send_sem.at[phase, peer], recv_sem=recv_sem.at[phase, me[axis]],
                device_id={axis: peer}, device_id_type=MESH,
            ).start()
            return carry

        lax.fori_loop(0, N_DEV - 1, one, 0)

    def wait_exchange(phase, axis, src, dst, what):
        def one(t, carry):
            peer = peer_of(axis, t)
            copy = pltpu.make_async_remote_copy(
                src_ref=src(peer), dst_ref=dst(peer),
                send_sem=send_sem.at[phase, peer], recv_sem=recv_sem.at[phase, peer],
                device_id={axis: peer}, device_id_type=MESH,
            )
            (copy.wait_recv if what == "recv" else copy.wait_send)()
            return carry

        lax.fori_loop(0, N_DEV - 1, one, 0)

    part = lambda ref: (lambda peer: ref.at[peer])
    whole = lambda ref: (lambda peer: ref)
    exchanges = {
        0: ("fsdp", part(c_send), part(c_recv)),
        1: ("fsdp", whole(s_send), part(s_recv)),
        2: ("dp", whole(cg_send), part(cg_recv)),
        3: ("fsdp", part(b_send), part(b_recv)),
        4: ("dp", part(l_send), part(l_recv)),
        5: ("dp", whole(bg_send), part(bg_recv)),
        6: ("fsdp", whole(m_send), part(m_recv)),
        7: ("dp", whole(n_send), part(n_recv)),
    }
    start = lambda phase: start_exchange(phase, *exchanges[phase])
    wait_recv = lambda phase: wait_exchange(phase, *exchanges[phase], "recv")
    wait_send = lambda phase: wait_exchange(phase, *exchanges[phase], "send")

    def load(slot):
        return pltpu.make_async_copy(fields.at[slot], fbuf.at[slot], load_sem.at[slot])

    for slot in range(slots):
        load(slot).start()

    barrier = pltpu.get_barrier_semaphore()
    for axis in ("fsdp", "dp"):
        def greet(t, carry, axis=axis):
            pl.semaphore_signal(barrier, inc=1, device_id={axis: peer_of(axis, t)}, device_id_type=MESH)
            return carry

        lax.fori_loop(0, N_DEV - 1, greet, 0)

    def x_phase(part_index, k1, plane):
        return xphase[part_index, k1 * length + me["fsdp"] * planes + plane]

    def fold_modes(slot, plane, product):
        direct = product[0:ROWS] + product[ROWS : 2 * ROWS]
        turned = product[2 * ROWS : 3 * ROWS] + product[3 * ROWS : 4 * ROWS]
        for k1 in range(MX):
            acc[slot, k1] += x_phase(0, k1, plane) * direct + x_phase(1, k1, plane) * turned

    def pack_modes(send):
        for k1 in range(MX):
            for k2 in range(MY):
                pieces = [acc[slot, k1, 4 * k2 : 4 * k2 + 4] for slot in range(slots)]
                send[k1 * MY + k2] = jnp.concatenate(pieces, axis=0)

    acc[...] = jnp.zeros_like(acc)
    for slot in range(slots):
        load(slot).wait()

        def forward_plane(plane, carry, slot=slot):
            fold_modes(slot, plane, dot(fwd_table[...], fbuf[slot, plane]))
            return carry

        lax.fori_loop(0, planes, forward_plane, 0)
    pack_modes(c_send)
    pl.semaphore_wait(barrier, 2 * (N_DEV - 1))
    start(0)
    c_recv[me["fsdp"]] = c_send[me["fsdp"]]

    rhs[...] = jnp.zeros_like(rhs)
    rhs[0:width, 0:width] = local_w[...]
    acc[...] = jnp.zeros_like(acc)
    local_acc[...] = jnp.zeros_like(local_acc)
    s_send[...] = jnp.zeros_like(s_send)
    grid_total = counts[0]
    for lane in range(1, N_DEV):
        grid_total = grid_total + counts[lane]
    scale = 1.0 / (jnp.zeros((1, width), jnp.float32) + grid_total.astype(jnp.float32))
    my_count = counts[me["dp"]]

    wait_recv(0)
    total = c_recv[0]
    for peer in range(1, N_DEV):
        total = total + c_recv[peer]
    coeff = (total * float(length) ** -1.5).astype(jnp.bfloat16)
    coeff_f = coeff.astype(jnp.float32)
    turned = times_i(coeff_f).astype(jnp.bfloat16)
    third = (lax.broadcasted_iota(jnp.int32, (rows, width), 0) // 2) % 2
    mixed = [dot(coeff, spec_w[k3, 0]) + dot(turned, spec_w[k3, 1]) for k3 in range(MZ)]
    s_send[0:rows] = jnp.where(third == 0, mixed[0], mixed[1]).astype(jnp.bfloat16)
    start(1)
    cg_send[...] = coeff_f
    start(2)
    s_recv[me["fsdp"]] = s_send[...]
    cg_recv[me["dp"]] = coeff_f
    wait_recv(1)

    for k1 in range(MX):
        owners = [s_recv[k1 * MY + k2].astype(jnp.float32) for k2 in range(MY)]
        for slot in range(slots):
            piece = jnp.concatenate([o[4 * slot : 4 * slot + 4] for o in owners], axis=0)
            acc_piece = times_i(piece)
            for plane in range(planes):
                term = x_phase(0, k1, plane) * piece + x_phase(1, k1, plane) * acc_piece
                if k1 == 0:
                    inv_rows[slot * planes + plane] = term
                else:
                    inv_rows[slot * planes + plane] += term

    chunks = cells // CHUNK
    picks = lax.broadcasted_iota(jnp.int32, (width, width), 0)

    def point(step, carry):
        unit = step // chunks
        slot, plane, piece = unit // planes, unit % planes, step % chunks
        first = pl.multiple_of(piece * CHUNK, CHUNK)
        live = jnp.int32(0)
        for j in range(slots):
            live = live + jnp.where(jnp.logical_and(lists[0, j] == slot, j < my_count), 1, 0)
        weight = proj[...] * scale * live.astype(jnp.float32)
        values = inv_rows[unit]
        high = values.astype(jnp.bfloat16)
        low = (values - high.astype(jnp.float32)).astype(jnp.bfloat16)
        rhs[width : width + 3 * ROWS, 0:width] = jnp.concatenate([high, high, low], axis=0)
        rhs[width : 2 * width, width : 2 * width] = jnp.where(picks == 3 * ROWS + unit, 1.0, 0.0).astype(jnp.bfloat16)
        field = fbuf[slot, plane, pl.ds(first, CHUNK)]
        left = jnp.concatenate([field, cell_table[pl.ds(first, CHUNK)]], axis=1)
        both = dot(left, rhs[...])
        pre, target = both[:, 0:width], both[:, width : 2 * width]
        gate = 0.5 * lax.erf(pre * ROOT_HALF) + 0.5
        bell = jnp.exp2(pre * pre * (-0.5 * LOG2_E))
        pred = jnp.sum(pre * gate * proj[...], axis=1, keepdims=True)
        slope = gate + pre * (bell * INV_ROOT_TWO_PI)
        d_pre = ((pred - target) * (slope * weight)).astype(jnp.bfloat16)
        local_acc[...] += dot_t(field, d_pre)
        fold_modes(slot, plane, dot(fwd_table[:, pl.ds(first, CHUNK)], d_pre))
        return carry

    lax.fori_loop(0, slots * planes * chunks, point, 0)

    for peer in range(N_DEV):
        l_send[peer] = local_acc[8 * peer : 8 * peer + 8]
    start(4)
    pack_modes(b_send)
    start(3)
    l_recv[me["dp"]] = l_send[me["dp"]]
    b_recv[me["fsdp"]] = b_send[me["fsdp"]]

    def sum_of(ref):
        value = ref[0]
        for peer in range(1, N_DEV):
            value = value + ref[peer]
        return value

    wait_recv(4)
    m_value = sum_of(l_recv)
    m_send[...] = m_value
    start(6)
    m_recv[me["fsdp"]] = m_value
    wait_recv(3)
    b_value = sum_of(b_recv) * float(MX * MY * MZ) ** -0.5
    bg_send[...] = b_value
    start(5)
    bg_recv[me["dp"]] = b_value
    wait_recv(6)
    n_value = sum_of(m_recv)
    n_send[...] = n_value
    start(7)
    n_recv[me["dp"]] = n_value

    wait_recv(2)
    wait_recv(5)
    every = N_DEV * rows
    coeff_all = cg_recv[...].reshape(every, width)
    back_all = bg_recv[...].reshape(every, width)
    third = (lax.broadcasted_iota(jnp.int32, (every, width), 0) // 2) % 2
    left = jnp.concatenate([jnp.where(third == k3, coeff_all, 0.0) for k3 in range(MZ)], axis=1)
    right = jnp.concatenate([back_all, -times_i(back_all)], axis=1)
    right_high = right.astype(jnp.bfloat16)
    right_low = (right - right_high.astype(jnp.float32)).astype(jnp.bfloat16)
    left = left.astype(jnp.bfloat16)
    grad = dot_t(left, right_high) + dot_t(left, right_low)
    for k3 in range(MZ):
        for part_index in range(2):
            out_spec[k3, part_index] = grad[
                k3 * width : (k3 + 1) * width, part_index * width : (part_index + 1) * width
            ]

    wait_recv(7)
    out_local[...] = n_recv[...].reshape(width, width)
    for phase in exchanges:
        wait_send(phase)


def body(fields, targets, lists, counts, spectral_w, local_w, proj):
    _, slots, planes, length, _, width = fields.shape
    cells = length * length
    rows = slots * 4
    xphase, fwd_table, inv_table = tables(length)
    target_rows = targets.reshape(slots * planes, cells).T
    pad = jnp.zeros((cells, width - 3 * ROWS - slots * planes), jnp.bfloat16)
    cell_table = jnp.concatenate([jnp.asarray(inv_table), target_rows, pad], axis=1)
    vmem = pl.BlockSpec(memory_space=pltpu.VMEM)
    smem = pl.BlockSpec(memory_space=pltpu.SMEM)
    f32, bf16 = jnp.float32, jnp.bfloat16
    gathered = pltpu.VMEM((N_DEV, rows, width), f32)
    eighth = pltpu.VMEM((N_DEV, 8, width), f32)
    return pl.pallas_call(
        functools.partial(kernel, length, slots, planes),
        out_shape=(
            jax.ShapeDtypeStruct(spectral_w.shape, f32),
            jax.ShapeDtypeStruct(local_w.shape, f32),
        ),
        in_specs=[pl.BlockSpec(memory_space=pl.ANY)] + [vmem] * 5 + [smem] * 3,
        out_specs=(vmem, vmem),
        scratch_shapes=[
            pltpu.VMEM((slots, planes, cells, width), bf16),
            pltpu.VMEM((2 * width, 2 * width), bf16),
            pltpu.VMEM((slots * planes, ROWS, width), f32),
            pltpu.VMEM((slots, MX, ROWS, width), f32),
            pltpu.VMEM((width, width), f32),
            gathered, gathered,
            pltpu.VMEM((32, width), bf16), pltpu.VMEM((N_DEV, 32, width), bf16),
            pltpu.VMEM((rows, width), f32), gathered,
            gathered, gathered,
            pltpu.VMEM((rows, width), f32), gathered,
            eighth, eighth,
            pltpu.VMEM((8, width), f32), eighth,
            pltpu.VMEM((8, width), f32), eighth,
            pltpu.SemaphoreType.DMA((slots,)),
            pltpu.SemaphoreType.DMA((8, N_DEV)),
            pltpu.SemaphoreType.DMA((8, N_DEV)),
        ],
        compiler_params=pltpu.CompilerParams(
            collective_id=0, has_side_effects=True, vmem_limit_bytes=60 * 1024 * 1024
        ),
        name="fno_step",
    )(
        fields.reshape(slots, planes, cells, width), cell_table, jnp.asarray(fwd_table), spectral_w, local_w,
        proj.reshape(1, width), lists, counts, jnp.asarray(xphase),
    )


def solution(mesh):
    return jax.shard_map(
        body,
        mesh=mesh,
        in_specs=(
            P("dp", None, "fsdp", None, None, None),
            P("dp", None, "fsdp", None),
            P("dp", None),
            P(),
            P("fsdp", None, None, None),
            P(),
            P(),
        ),
        out_specs=(P("fsdp", None, None, None), P()),
        check_vma=False,
    )
```

```python
import functools
import math

import jax
import jax.numpy as jnp
import numpy as np
from jax import lax
from jax.experimental import pallas as pl
from jax.experimental.pallas import tpu as pltpu
from jax.sharding import PartitionSpec as P

MX, MY, MZ = 4, 4, 2
N_DEV = 16
ROWS = MY * MZ * 2
ROOT_HALF = 0.7071067811865476
INV_ROOT_TWO_PI = 0.3989422804014327
LOG2_E = 1.4426950408889634
MESH = pl.DeviceIdType.MESH
PART = 1152
SHARED = 2


def phases(ids, length):
    product = (ids[:, None] * np.arange(length)[None, :]) % length
    angle = product.astype(np.float32) * np.float32(2.0 * math.pi / length)
    return np.cos(angle).astype(np.float32), np.sin(angle).astype(np.float32)


def split_bf16(values):
    high = values.astype(jnp.bfloat16)
    low = (values - high.astype(np.float32)).astype(jnp.bfloat16)
    return high, low


@functools.lru_cache(maxsize=None)
def tables(length):
    cos_x, sin_x = phases(np.arange(MX) - MX // 2, length)
    cos_y, sin_y = phases(np.arange(MY) - MY // 2, length)
    cos_z, sin_z = phases(np.arange(MZ), length)
    round_z = lambda t: t.astype(jnp.bfloat16).astype(np.float32)

    def product(cz, sz):
        re = cos_y[:, None, :, None] * cz[None, :, None, :] - sin_y[:, None, :, None] * sz[None, :, None, :]
        im = sin_y[:, None, :, None] * cz[None, :, None, :] + cos_y[:, None, :, None] * sz[None, :, None, :]
        shape = (MY, MZ, length * length)
        return re.reshape(shape), -im.reshape(shape)

    re, im = product(round_z(cos_z), round_z(sin_z))
    forward = np.concatenate(split_bf16(np.stack([re, im], axis=2).reshape(ROWS, -1)), axis=0)
    re, im = product(cos_z, sin_z)
    back = np.stack([re, im], axis=2).reshape(ROWS, -1) * np.float32(float(MX * MY * MZ) ** -0.5)
    high, low = split_bf16(back)
    inverse = np.concatenate([high, low, high], axis=0)
    return np.stack([cos_x, sin_x]).reshape(2, -1), forward, inverse


def times_i(values):
    rows, width = values.shape
    grouped = values.reshape(rows // 8, 8, width)
    even = lax.broadcasted_iota(jnp.int32, grouped.shape, 1) % 2 == 0
    turned = jnp.where(even, -pltpu.roll(grouped, 7, 1), pltpu.roll(grouped, 1, 1))
    return turned.reshape(rows, width)


def dot(a, b):
    return jnp.dot(a, b, preferred_element_type=jnp.float32)


def kernel(
    length, slots, planes,
    fields, targets, inv_table, fwd_table, spec_w, local_w, proj, lists, counts, xphase,
    out_spec, out_local,
    fbuf, pbuf, f_share, d_buf, cell_table, rhs, inv_rows, inv_share, tgt, tgt_send, tgt_share, acc, local_acc,
    c_send, c_recv, s_send, s_recv, cg_send, cg_recv, b_send, b_recv, bg_send, bg_recv,
    l_send, l_recv, m_send, m_recv, n_send, n_recv,
    load_sem, send_sem, recv_sem, share_send_sem, share_recv_sem,
):
    cells = length * length
    width = fields.shape[-1]
    rows = slots * 4
    work = slots - SHARED
    units = work * planes
    half = units // 2
    parts = cells // PART
    me = {"fsdp": lax.axis_index("fsdp"), "dp": lax.axis_index("dp")}
    partner = me["dp"] + 1 - 2 * lax.rem(me["dp"], 2)
    order = [lists[0, j] for j in range(slots)]
    my_count, partner_count = counts[me["dp"]], counts[partner]
    mine = my_count > 2
    shared_live = jnp.maximum(my_count, partner_count) > 2

    def peer_of(axis, t):
        offset = 8 + ((t + 1) // 2) * (1 - 2 * (t % 2))
        return lax.rem(me[axis] + offset, N_DEV)

    exchanges = {
        0: ("fsdp", lambda peer: c_send.at[peer], c_recv),
        1: ("fsdp", lambda peer: s_send, s_recv),
        2: ("dp", lambda peer: cg_send, cg_recv),
        3: ("fsdp", lambda peer: b_send.at[peer], b_recv),
        4: ("dp", lambda peer: l_send.at[peer], l_recv),
        5: ("dp", lambda peer: bg_send, bg_recv),
        6: ("fsdp", lambda peer: m_send, m_recv),
        7: ("dp", lambda peer: n_send, n_recv),
    }

    def start(phase):
        axis, src, landing = exchanges[phase]

        def one(t, carry):
            peer = peer_of(axis, t)
            pltpu.make_async_remote_copy(
                src_ref=src(peer), dst_ref=landing.at[me[axis]],
                send_sem=send_sem.at[phase], recv_sem=recv_sem.at[phase],
                device_id={axis: peer}, device_id_type=MESH,
            ).start()
            return carry

        lax.fori_loop(0, N_DEV - 1, one, 0)

    def all_of(phase):
        axis, _, landing = exchanges[phase]
        bytes_of_all = landing.at[pl.ds(0, N_DEV - 1)]
        return pltpu.make_async_remote_copy(
            src_ref=bytes_of_all, dst_ref=bytes_of_all,
            send_sem=send_sem.at[phase], recv_sem=recv_sem.at[phase],
            device_id={axis: peer_of(axis, 0)}, device_id_type=MESH,
        )

    wait_recv = lambda phase: all_of(phase).wait_recv()
    wait_send = lambda phase: all_of(phase).wait_send()

    def share(index, src, dst):
        return pltpu.make_async_remote_copy(
            src_ref=src, dst_ref=dst,
            send_sem=share_send_sem.at[index], recv_sem=share_recv_sem.at[index],
            device_id={"dp": partner}, device_id_type=MESH,
        )

    shares = [
        share(0, tgt_send, tgt_share),
        share(1, pbuf.at[pl.ds(work, SHARED)], f_share),
        share(2, inv_rows.at[pl.ds(units, SHARED * planes)], inv_share),
    ]

    def load(slot):
        return pltpu.make_async_copy(fields.at[slot], fbuf.at[slot], load_sem.at[slot])

    for slot in range(slots):
        load(slot).start()

    barrier = pltpu.get_barrier_semaphore()
    for axis in ("fsdp", "dp"):
        def greet(t, carry, axis=axis):
            pl.semaphore_signal(barrier, inc=1, device_id={axis: peer_of(axis, t)}, device_id_type=MESH)
            return carry

        lax.fori_loop(0, N_DEV - 1, greet, 0)

    def x_phase(part_index, k1, plane):
        return xphase[part_index, k1 * length + me["fsdp"] * planes + plane]

    def fold_modes(slot, plane, product):
        direct = product[0:ROWS] + product[ROWS : 2 * ROWS]
        turned = times_i(direct)
        for k1 in range(MX):
            acc[slot, k1] += x_phase(0, k1, plane) * direct - x_phase(1, k1, plane) * turned

    def pack_modes(send, picks):
        for k1 in range(MX):
            for k2 in range(MY):
                send[k1 * MY + k2] = jnp.concatenate([acc[p, k1, 4 * k2 : 4 * k2 + 4] for p in picks], axis=0)

    acc[...] = jnp.zeros_like(acc)
    for slot in range(slots):
        load(slot).wait()

        def forward_plane(plane, carry, slot=slot):
            fold_modes(slot, plane, dot(fwd_table[...], fbuf[slot, plane]))
            return carry

        lax.fori_loop(0, planes, forward_plane, 0)
    pack_modes(c_send, order)
    pl.semaphore_wait(barrier, 2 * (N_DEV - 1))
    start(0)

    tgt[...] = jnp.zeros_like(tgt)
    tgt_send[...] = jnp.zeros_like(tgt_send)
    for j in range(SHARED):
        tgt_send[planes * j : planes * (j + 1)] = targets[order[work + j]].astype(jnp.float32)
    shares[0].start()

    def by_position(j):
        def one(plane, carry):
            pbuf[j, plane] = fbuf[order[j], plane]
            return carry

        lax.fori_loop(0, planes, one, 0)

    for j in range(work, slots):
        by_position(j)
    shares[1].start()
    c_recv[me["fsdp"]] = c_send[me["fsdp"]]
    for j in range(work):
        tgt[planes * j : planes * (j + 1)] = targets[order[j]].astype(jnp.float32)
        by_position(j)
    rhs[...] = jnp.zeros_like(rhs)
    rhs[0:width, 0:width] = local_w[...]
    acc[...] = jnp.zeros_like(acc)
    local_acc[...] = jnp.zeros_like(local_acc)
    d_buf[...] = jnp.zeros_like(d_buf)
    s_send[...] = jnp.zeros_like(s_send)
    grid_total = counts[0]
    for lane in range(1, N_DEV):
        grid_total = grid_total + counts[lane]
    scale = 1.0 / (jnp.zeros((1, width), jnp.float32) + grid_total.astype(jnp.float32))
    shares[0].wait_recv()
    tgt[half : 2 * half] = jnp.where(mine, tgt[half : 2 * half], tgt_share[0:half])
    cell_rows = jnp.concatenate(
        [inv_table[...], tgt[...].astype(jnp.bfloat16), jnp.zeros((width - 3 * ROWS - 16, cells), jnp.bfloat16)], axis=0
    )
    cell_table[...] = cell_rows.T

    wait_recv(0)
    total = c_recv[0]
    for peer in range(1, N_DEV):
        total = total + c_recv[peer]
    coeff = (total * float(length) ** -1.5).astype(jnp.bfloat16)
    coeff_f = coeff.astype(jnp.float32)
    turned = times_i(coeff_f).astype(jnp.bfloat16)
    third = (lax.broadcasted_iota(jnp.int32, (rows, width), 0) // 2) % 2
    mixed = [dot(coeff, spec_w[k3, 0]) + dot(turned, spec_w[k3, 1]) for k3 in range(MZ)]
    s_send[0:rows] = jnp.where(third == 0, mixed[0], mixed[1]).astype(jnp.bfloat16)
    start(1)
    cg_send[...] = coeff_f
    start(2)
    s_recv[me["fsdp"]] = s_send[...]
    cg_recv[me["dp"]] = coeff_f
    wait_recv(1)

    for k1 in range(MX):
        owners = [s_recv[k1 * MY + k2].astype(jnp.float32) for k2 in range(MY)]
        for j in range(slots):
            piece = jnp.concatenate([o[4 * j : 4 * j + 4] for o in owners], axis=0)
            turned_piece = times_i(piece)
            for plane in range(planes):
                term = x_phase(0, k1, plane) * piece + x_phase(1, k1, plane) * turned_piece
                if k1 == 0:
                    inv_rows[j * planes + plane] = term
                else:
                    inv_rows[j * planes + plane] += term
    shares[2].start()

    picks = lax.broadcasted_iota(jnp.int32, (width, width), 0)

    def reduce_part(unit, part_index):
        slot, plane = unit // planes, unit % planes
        rows_here = pl.ds(part_index * PART, PART)
        left = jnp.concatenate([pbuf[slot, plane, rows_here].T, fwd_table[:, rows_here]], axis=0)
        product = dot(left, d_buf[part_index])
        local_acc[...] += product[0:width]
        fold_modes(slot, plane, product[width:])

    def point(unit, carry):
        @pl.when(unit == half)
        def _():
            shares[1].wait_recv()
            shares[2].wait_recv()
            inv_rows[half:units] = jnp.where(mine, inv_rows[half:units], inv_share[0:half])

            def one(k, carry):
                slot, plane = k // planes, k % planes
                own = pbuf[work // 2 + slot, plane]
                pbuf[work // 2 + slot, plane] = jnp.where(mine, own, f_share[slot, plane])
                return carry

            lax.fori_loop(0, half, one, 0)

        slot, plane = unit // planes, unit % planes
        live = jnp.where(slot < work // 2, jnp.where(slot < my_count, 1, 0), jnp.where(shared_live, 1, 0))
        weight = proj[...] * scale * live.astype(jnp.float32)
        half_proj, half_weight, bell_weight = 0.5 * proj[...], 0.5 * weight, INV_ROOT_TWO_PI * weight
        values = inv_rows[unit]
        high = values.astype(jnp.bfloat16)
        low = (values - high.astype(jnp.float32)).astype(jnp.bfloat16)
        rhs[width : width + 3 * ROWS, 0:width] = jnp.concatenate([high, high, low], axis=0)
        rhs[width : 2 * width, width : 2 * width] = jnp.where(picks == 3 * ROWS + unit, 1.0, 0.0).astype(jnp.bfloat16)
        for part_index in range(parts):
            rows_here = pl.ds(part_index * PART, PART)
            left = jnp.concatenate([pbuf[slot, plane, rows_here], cell_table[rows_here]], axis=1)
            both = dot(left, rhs[...])
            pre, target = both[:, 0:width], both[:, width : 2 * width]
            gate = lax.erf(pre * ROOT_HALF) + 1.0
            bell = jnp.exp2(pre * pre * (-0.5 * LOG2_E))
            pred = jnp.sum(pre * gate * half_proj, axis=1, keepdims=True)
            slope = gate * half_weight + pre * bell * bell_weight
            d_buf[part_index] = ((pred - target) * slope).astype(jnp.bfloat16)
            if part_index == 0:
                reduce_part(jnp.maximum(unit - 1, 0), parts - 1)
            else:
                reduce_part(unit, part_index - 1)
        return carry

    lax.fori_loop(0, units, point, 0)
    reduce_part(units - 1, parts - 1)

    for peer in range(N_DEV):
        l_send[peer] = local_acc[8 * peer : 8 * peer + 8]
    start(4)
    pack_modes(b_send, range(work))
    start(3)
    l_recv[me["dp"]] = l_send[me["dp"]]
    b_recv[me["fsdp"]] = b_send[me["fsdp"]]

    def sum_of(ref):
        value = ref[0]
        for peer in range(1, N_DEV):
            value = value + ref[peer]
        return value

    wait_recv(4)
    m_value = sum_of(l_recv)
    m_send[...] = m_value
    start(6)
    m_recv[me["fsdp"]] = m_value
    wait_recv(3)
    b_value = sum_of(b_recv) * float(MX * MY * MZ) ** -0.5
    bg_send[...] = b_value
    start(5)
    bg_recv[me["dp"]] = b_value

    wait_recv(2)
    near, far = 4 * (work // 2), 4 * work
    pieces = []
    for lane in range(N_DEV):
        kept = jnp.where(counts[lane] > 2, cg_recv[lane, near:far], cg_recv[lane ^ 1, far:rows])
        pieces += [cg_recv[lane, 0:near], kept]
    coeff_all = jnp.concatenate(pieces, axis=0)
    every = N_DEV * far
    third = (lax.broadcasted_iota(jnp.int32, (every, width), 0) // 2) % 2
    left = jnp.concatenate([jnp.where(third == k3, coeff_all, 0.0) for k3 in range(MZ)], axis=1)
    left = left.astype(jnp.bfloat16).T

    wait_recv(6)
    n_value = sum_of(m_recv)
    n_send[...] = n_value
    start(7)
    n_recv[me["dp"]] = n_value

    wait_recv(5)
    back_all = bg_recv[...].reshape(every, width)
    right = jnp.concatenate([back_all, -times_i(back_all)], axis=1)
    right_high = right.astype(jnp.bfloat16)
    right_low = (right - right_high.astype(jnp.float32)).astype(jnp.bfloat16)
    grad = dot(left, right_high) + dot(left, right_low)
    for k3 in range(MZ):
        for part_index in range(2):
            out_spec[k3, part_index] = grad[
                k3 * width : (k3 + 1) * width, part_index * width : (part_index + 1) * width
            ]

    wait_recv(7)
    out_local[...] = n_recv[...].reshape(width, width)
    for phase in exchanges:
        wait_send(phase)
    for one in shares:
        one.wait_send()


def copy_out(spec_in, local_in, out_spec, out_local):
    out_spec[...] = spec_in[...]
    out_local[...] = local_in[...]


def body(fields, targets, lists, counts, spectral_w, local_w, proj):
    _, slots, planes, length, _, width = fields.shape
    cells = length * length
    rows = slots * 4
    work = slots - SHARED
    xphase, fwd_table, inv_table = tables(length)
    vmem = pl.BlockSpec(memory_space=pltpu.VMEM)
    smem = pl.BlockSpec(memory_space=pltpu.SMEM)
    f32, bf16 = jnp.float32, jnp.bfloat16
    coeffs = pltpu.VMEM((N_DEV, rows, width), f32)
    backs = pltpu.VMEM((N_DEV, 4 * work, width), f32)
    eighth = pltpu.VMEM((N_DEV, 8, width), f32)
    results = (
        jax.ShapeDtypeStruct(spectral_w.shape, f32),
        jax.ShapeDtypeStruct(local_w.shape, f32),
    )
    grads = pl.pallas_call(
        functools.partial(kernel, length, slots, planes),
        out_shape=results,
        in_specs=[pl.BlockSpec(memory_space=pl.ANY)] + [vmem] * 6 + [smem] * 3,
        out_specs=(vmem, vmem),
        scratch_shapes=[
            pltpu.VMEM((slots, planes, cells, width), bf16),
            pltpu.VMEM((slots, planes, cells, width), bf16),
            pltpu.VMEM((SHARED, planes, cells, width), bf16),
            pltpu.VMEM((cells // PART, PART, width), bf16),
            pltpu.VMEM((cells, width), bf16),
            pltpu.VMEM((2 * width, 2 * width), bf16),
            pltpu.VMEM((slots * planes, ROWS, width), f32),
            pltpu.VMEM((SHARED * planes, ROWS, width), f32),
            pltpu.VMEM((16, cells), f32), pltpu.VMEM((8, cells), f32), pltpu.VMEM((8, cells), f32),
            pltpu.VMEM((slots, MX, ROWS, width), f32),
            pltpu.VMEM((width, width), f32),
            coeffs, coeffs,
            pltpu.VMEM((32, width), bf16), pltpu.VMEM((N_DEV, 32, width), bf16),
            pltpu.VMEM((rows, width), f32), coeffs,
            backs, backs,
            pltpu.VMEM((4 * work, width), f32), backs,
            eighth, eighth,
            pltpu.VMEM((8, width), f32), eighth,
            pltpu.VMEM((8, width), f32), eighth,
            pltpu.SemaphoreType.DMA((slots,)),
            pltpu.SemaphoreType.DMA((8,)),
            pltpu.SemaphoreType.DMA((8,)),
            pltpu.SemaphoreType.DMA((3,)),
            pltpu.SemaphoreType.DMA((3,)),
        ],
        compiler_params=pltpu.CompilerParams(
            collective_id=0, has_side_effects=True, vmem_limit_bytes=48 * 1024 * 1024
        ),
        name="fno_step",
    )(
        fields.reshape(slots, planes, cells, width), targets.reshape(slots, planes, cells),
        jnp.asarray(inv_table), jnp.asarray(fwd_table), spectral_w, local_w,
        proj.reshape(1, width), lists, counts, jnp.asarray(xphase),
    )
    return pl.pallas_call(
        copy_out, out_shape=results, in_specs=[vmem, vmem], out_specs=(vmem, vmem), name="copy_out",
        compiler_params=pltpu.CompilerParams(vmem_limit_bytes=2 * 1024 * 1024),
    )(*grads)


def solution(mesh):
    return jax.shard_map(
        body,
        mesh=mesh,
        in_specs=(
            P("dp", None, "fsdp", None, None, None),
            P("dp", None, "fsdp", None),
            P("dp", None),
            P(),
            P("fsdp", None, None, None),
            P(),
            P(),
        ),
        out_specs=(P("fsdp", None, None, None), P()),
        check_vma=False,
    )
```

```python
import functools
import math

import jax
import jax.numpy as jnp
import numpy as np
from jax import lax
from jax.experimental import pallas as pl
from jax.experimental.pallas import tpu as pltpu
from jax.sharding import PartitionSpec as P

MX, MY, MZ = 4, 4, 2
N_DEV = 16
ROWS = MY * MZ * 2
ROOT_HALF = 0.7071067811865476
INV_ROOT_TWO_PI = 0.3989422804014327
LOG2_E = 1.4426950408889634
MESH = pl.DeviceIdType.MESH
PART = 1152
UNROLL = 2
INPUTS = 9
SHARED = 2


def phases(ids, length):
    product = (ids[:, None] * np.arange(length)[None, :]) % length
    angle = product.astype(np.float32) * np.float32(2.0 * math.pi / length)
    return np.cos(angle).astype(np.float32), np.sin(angle).astype(np.float32)


def split_bf16(values):
    high = values.astype(jnp.bfloat16)
    low = (values - high.astype(np.float32)).astype(jnp.bfloat16)
    return high, low


@functools.lru_cache(maxsize=None)
def tables(length):
    cos_x, sin_x = phases(np.arange(MX) - MX // 2, length)
    cos_y, sin_y = phases(np.arange(MY) - MY // 2, length)
    cos_z, sin_z = phases(np.arange(MZ), length)
    round_z = lambda t: t.astype(jnp.bfloat16).astype(np.float32)

    def product(cz, sz):
        re = cos_y[:, None, :, None] * cz[None, :, None, :] - sin_y[:, None, :, None] * sz[None, :, None, :]
        im = sin_y[:, None, :, None] * cz[None, :, None, :] + cos_y[:, None, :, None] * sz[None, :, None, :]
        shape = (MY, MZ, length * length)
        return re.reshape(shape), -im.reshape(shape)

    re, im = product(round_z(cos_z), round_z(sin_z))
    forward = np.concatenate(split_bf16(np.stack([re, im], axis=2).reshape(ROWS, -1)), axis=0)
    re, im = product(cos_z, sin_z)
    back = np.stack([re, im], axis=2).reshape(ROWS, -1) * np.float32(float(MX * MY * MZ) ** -0.5)
    high, low = split_bf16(back)
    inverse = np.concatenate([high, low, high], axis=0)
    return np.stack([cos_x, sin_x]).reshape(2, -1), forward, inverse


def times_i(values):
    rows, width = values.shape
    grouped = values.reshape(rows // 8, 8, width)
    even = lax.broadcasted_iota(jnp.int32, grouped.shape, 1) % 2 == 0
    turned = jnp.where(even, -pltpu.roll(grouped, 7, 1), pltpu.roll(grouped, 1, 1))
    return turned.reshape(rows, width)


def dot(a, b):
    return jnp.dot(a, b, preferred_element_type=jnp.float32)


def kernel(
    length, slots, planes,
    fields, *rest,
):
    inputs, (out_spec, out_local), rest = rest[:INPUTS], rest[INPUTS : INPUTS + 2], rest[INPUTS + 2 :]
    kept, rest = rest[:INPUTS], rest[INPUTS:]
    fwd_table, xphase, lists, counts, targets, inv_table, local_w, proj, spec_w = kept
    (
    fbuf, pbuf, f_share, d_buf, cell_table, rhs, inv_rows, inv_share, tgt, tgt_send, tgt_share, acc, local_acc,
    ca_send, ca_recv, cb_send, cb_recv, sa_send, sa_recv, sb_send, sb_recv, cg_send, cg_recv,
    ba_send, ba_recv, bb_send, bb_recv, bg_send, bg_recv,
    l_recv, m_send, m_recv, n_send, n_recv,
    load_sem, send_sem, recv_sem, share_send_sem, share_recv_sem,
    ) = rest
    cells = length * length
    width = fields.shape[-1]
    near = slots - 2 * SHARED
    work = slots - SHARED
    units = work * planes
    half = units // 2
    parts = cells // PART
    me = {"fsdp": lax.axis_index("fsdp"), "dp": lax.axis_index("dp")}
    partner = me["dp"] + 1 - 2 * lax.rem(me["dp"], 2)
    offsets = [8 + ((t + 1) // 2) * (1 - 2 * (t % 2)) for t in range(N_DEV - 1)]

    def peer_of(axis, t):
        return lax.rem(me[axis] + offsets[t], N_DEV)

    exchanges = {
        0: ("fsdp", lambda peer: ca_send.at[peer], ca_recv),
        1: ("fsdp", lambda peer: sa_send, sa_recv),
        2: ("dp", lambda peer: cg_send, cg_recv),
        3: ("fsdp", lambda peer: ba_send.at[peer], ba_recv),
        4: ("dp", lambda peer: local_acc.at[peer], l_recv),
        5: ("dp", lambda peer: bg_send, bg_recv),
        6: ("fsdp", lambda peer: m_send, m_recv),
        7: ("dp", lambda peer: n_send, n_recv),
        8: ("fsdp", lambda peer: cb_send.at[peer], cb_recv),
        9: ("fsdp", lambda peer: sb_send, sb_recv),
        10: ("fsdp", lambda peer: bb_send.at[peer], bb_recv),
    }

    def start(phase):
        axis, src, landing = exchanges[phase]
        for t in range(N_DEV - 1):
            peer = peer_of(axis, t)
            pltpu.make_async_remote_copy(
                src_ref=src(peer), dst_ref=landing.at[me[axis]],
                send_sem=send_sem.at[phase], recv_sem=recv_sem.at[phase],
                device_id={axis: peer}, device_id_type=MESH,
            ).start()

    def all_of(phase):
        axis, _, landing = exchanges[phase]
        bytes_of_all = landing.at[pl.ds(0, N_DEV - 1)]
        return pltpu.make_async_remote_copy(
            src_ref=bytes_of_all, dst_ref=bytes_of_all,
            send_sem=send_sem.at[phase], recv_sem=recv_sem.at[phase],
            device_id={axis: peer_of(axis, 0)}, device_id_type=MESH,
        )

    wait_recv = lambda phase: all_of(phase).wait_recv()
    wait_send = lambda phase: all_of(phase).wait_send()

    def share(index, src, dst):
        return pltpu.make_async_remote_copy(
            src_ref=src, dst_ref=dst,
            send_sem=share_send_sem.at[index], recv_sem=share_recv_sem.at[index],
            device_id={"dp": partner}, device_id_type=MESH,
        )

    shares = [
        share(0, tgt_send, tgt_share),
        share(1, pbuf.at[pl.ds(work, SHARED)], f_share),
        share(2, inv_rows.at[pl.ds(units, SHARED * planes)], inv_share),
    ]

    def load(slot):
        return pltpu.make_async_copy(fields.at[slot], fbuf.at[slot], load_sem.at[slot])

    fetches = [
        pltpu.make_async_copy(src, dst, load_sem.at[slots + index]) for index, (src, dst) in enumerate(zip(inputs, kept))
    ]
    for fetch in fetches[:4]:
        fetch.start()
    for slot in range(slots):
        load(slot).start()
    for fetch in fetches[4:]:
        fetch.start()

    barrier = pltpu.get_barrier_semaphore()
    for t in range(N_DEV - 1):
        for axis in ("fsdp", "dp"):
            pl.semaphore_signal(barrier, inc=1, device_id={axis: peer_of(axis, t)}, device_id_type=MESH)

    def x_phase(part_index, k1, plane):
        return xphase[part_index, k1 * length + me["fsdp"] * planes + plane]

    def fold_modes(slot, plane, product):
        direct = product[0:ROWS] + product[ROWS : 2 * ROWS]
        turned = times_i(direct)
        for k1 in range(MX):
            acc[slot, k1] += x_phase(0, k1, plane) * direct - x_phase(1, k1, plane) * turned

    def pack_modes(send, picks):
        for k1 in range(MX):
            for k2 in range(MY):
                send[k1 * MY + k2] = jnp.concatenate([acc[p, k1, 4 * k2 : 4 * k2 + 4] for p in picks], axis=0)

    acc[...] = jnp.zeros_like(acc)
    for fetch in fetches[:4]:
        fetch.wait()
    order = [lists[0, j] for j in range(slots)]
    my_count, partner_count = counts[me["dp"]], counts[partner]
    mine = my_count > 2
    shared_live = jnp.maximum(my_count, partner_count) > 2

    for slot in range(slots):
        load(slot).wait()

        def forward_plane(plane, carry, slot=slot):
            fold_modes(slot, plane, dot(fwd_table[...], fbuf[slot, plane]))
            return carry

        lax.fori_loop(0, planes, forward_plane, 0)
    pack_modes(ca_send, order[:near])
    pl.semaphore_wait(barrier, 2 * (N_DEV - 1))
    start(0)
    pack_modes(cb_send, order[near:])
    start(8)

    for fetch in fetches[4:]:
        fetch.wait()
    tgt[...] = jnp.zeros_like(tgt)
    tgt_send[...] = jnp.zeros_like(tgt_send)
    for j in range(SHARED):
        tgt_send[planes * j : planes * (j + 1)] = targets[order[work + j]].astype(jnp.float32)
    shares[0].start()

    def by_position(j):
        def one(plane, carry):
            pbuf[j, plane] = fbuf[order[j], plane]
            return carry

        lax.fori_loop(0, planes, one, 0)

    for j in range(work, slots):
        by_position(j)
    shares[1].start()
    ca_recv[me["fsdp"]] = ca_send[me["fsdp"]]
    cb_recv[me["fsdp"]] = cb_send[me["fsdp"]]
    for j in range(work):
        tgt[planes * j : planes * (j + 1)] = targets[order[j]].astype(jnp.float32)
        by_position(j)
    rhs[...] = jnp.zeros_like(rhs)
    rhs[0:width, 0:width] = local_w[...]
    acc[...] = jnp.zeros_like(acc)
    local_acc[...] = jnp.zeros_like(local_acc)
    d_buf[...] = jnp.zeros_like(d_buf)
    grid_total = counts[0]
    for lane in range(1, N_DEV):
        grid_total = grid_total + counts[lane]
    scale = 1.0 / (jnp.zeros((1, width), jnp.float32) + grid_total.astype(jnp.float32))
    shares[0].wait_recv()
    tgt[half : 2 * half] = jnp.where(mine, tgt[half : 2 * half], tgt_share[0:half])
    cell_rows = jnp.concatenate(
        [inv_table[...], tgt[...].astype(jnp.bfloat16), jnp.zeros((width - 3 * ROWS - 16, cells), jnp.bfloat16)], axis=0
    )
    cell_table[...] = cell_rows.T

    def sum_of(ref):
        value = ref[0]
        for peer in range(1, N_DEV):
            value = value + ref[peer]
        return value

    def mix(landing, send):
        coeff = (sum_of(landing) * float(length) ** -1.5).astype(jnp.bfloat16)
        coeff_f = coeff.astype(jnp.float32)
        turned = times_i(coeff_f).astype(jnp.bfloat16)
        third = (lax.broadcasted_iota(jnp.int32, coeff.shape, 0) // 2) % 2
        mixed = [dot(coeff, spec_w[k3, 0]) + dot(turned, spec_w[k3, 1]) for k3 in range(MZ)]
        send[...] = jnp.where(third == 0, mixed[0], mixed[1]).astype(jnp.bfloat16)
        return coeff_f

    wait_recv(0)
    coeff_near = mix(ca_recv, sa_send)
    start(1)
    wait_recv(8)
    coeff_far = mix(cb_recv, sb_send)
    start(9)
    cg_send[...] = jnp.concatenate([coeff_near, coeff_far], axis=0)
    start(2)
    sa_recv[me["fsdp"]] = sa_send[...]
    sb_recv[me["fsdp"]] = sb_send[...]
    cg_recv[me["dp"]] = cg_send[...]

    def inverse_rows(landing, first, last):
        for k1 in range(MX):
            owners = [landing[k1 * MY + k2].astype(jnp.float32) for k2 in range(MY)]
            for j in range(last - first):
                piece = jnp.concatenate([o[4 * j : 4 * j + 4] for o in owners], axis=0)
                turned_piece = times_i(piece)
                for plane in range(planes):
                    term = x_phase(0, k1, plane) * piece + x_phase(1, k1, plane) * turned_piece
                    unit = (first + j) * planes + plane
                    if k1 == 0:
                        inv_rows[unit] = term
                    else:
                        inv_rows[unit] += term

    wait_recv(1)
    inverse_rows(sa_recv, 0, near)

    picks = lax.broadcasted_iota(jnp.int32, (width, width), 0)

    def reduce_part(unit, part_index):
        slot, plane = unit // planes, unit % planes
        rows_here = pl.ds(part_index * PART, PART)
        left = jnp.concatenate([pbuf[slot, plane, rows_here].T, fwd_table[:, rows_here]], axis=0)
        product = dot(left, d_buf[part_index])
        local_acc[...] += product[0:width].reshape(local_acc.shape)
        fold_modes(slot, plane, product[width:])

    def point(unit):
        slot, plane = unit // planes, unit % planes
        live = jnp.where(slot < near, jnp.where(slot < my_count, 1, 0), jnp.where(shared_live, 1, 0))
        weight = proj[...] * scale * live.astype(jnp.float32)
        half_proj, half_weight, bell_weight = 0.5 * proj[...], 0.5 * weight, INV_ROOT_TWO_PI * weight
        values = inv_rows[unit]
        high = values.astype(jnp.bfloat16)
        low = (values - high.astype(jnp.float32)).astype(jnp.bfloat16)
        rhs[width : width + 3 * ROWS, 0:width] = jnp.concatenate([high, high, low], axis=0)
        rhs[width : 2 * width, width : 2 * width] = jnp.where(picks == 3 * ROWS + unit, 1.0, 0.0).astype(jnp.bfloat16)
        for part_index in range(parts):
            rows_here = pl.ds(part_index * PART, PART)
            left = jnp.concatenate([pbuf[slot, plane, rows_here], cell_table[rows_here]], axis=1)
            both = dot(left, rhs[...])
            pre, target = both[:, 0:width], both[:, width : 2 * width]
            gate = lax.erf(pre * ROOT_HALF) + 1.0
            bell = jnp.exp2(pre * pre * (-0.5 * LOG2_E))
            pred = jnp.sum(pre * gate * half_proj, axis=1, keepdims=True)
            slope = gate * half_weight + pre * bell * bell_weight
            d_buf[part_index] = ((pred - target) * slope).astype(jnp.bfloat16)
            if part_index == 0:
                reduce_part(jnp.maximum(unit - 1, 0), parts - 1)
            else:
                reduce_part(unit, part_index - 1)

    def step(index, carry):
        first = index * UNROLL

        @pl.when(first == 4)
        def _():
            wait_recv(9)
            inverse_rows(sb_recv, near, slots)
            shares[2].start()

        @pl.when(first == half)
        def _():
            shares[1].wait_recv()
            shares[2].wait_recv()
            inv_rows[half:units] = jnp.where(mine, inv_rows[half:units], inv_share[0:half])

            def one(k, carry):
                slot, plane = k // planes, k % planes
                pbuf[near + slot, plane] = jnp.where(mine, pbuf[near + slot, plane], f_share[slot, plane])
                return carry

            lax.fori_loop(0, half, one, 0)

        @pl.when(first == half + 2)
        def _():
            pack_modes(ba_send, range(near))
            start(3)
            ba_recv[me["fsdp"]] = ba_send[me["fsdp"]]

        for sub in range(UNROLL):
            point(first + sub)
        return carry

    lax.fori_loop(0, units // UNROLL, step, 0)
    reduce_part(units - 1, parts - 1)

    start(4)
    pack_modes(bb_send, range(near, work))
    start(10)
    l_recv[me["dp"]] = local_acc[me["dp"]]
    bb_recv[me["fsdp"]] = bb_send[me["fsdp"]]
    back_scale = float(MX * MY * MZ) ** -0.5
    wait_recv(3)
    near_value = sum_of(ba_recv) * back_scale

    wait_recv(4)
    m_value = sum_of(l_recv)
    m_send[...] = m_value
    start(6)
    m_recv[me["fsdp"]] = m_value
    wait_recv(10)
    bg_send[...] = jnp.concatenate([near_value, sum_of(bb_recv) * back_scale], axis=0)
    start(5)
    bg_recv[me["dp"]] = bg_send[...]

    wait_recv(2)
    first, far = 4 * near, 4 * work
    pieces = []
    for lane in range(N_DEV):
        taken = jnp.where(counts[lane] > 2, cg_recv[lane, first:far], cg_recv[lane ^ 1, far : 4 * slots])
        pieces += [cg_recv[lane, 0:first], taken]
    coeff_all = jnp.concatenate(pieces, axis=0)
    every = N_DEV * far
    third = (lax.broadcasted_iota(jnp.int32, (every, width), 0) // 2) % 2
    left = jnp.concatenate([jnp.where(third == k3, coeff_all, 0.0) for k3 in range(MZ)], axis=1)
    left = left.astype(jnp.bfloat16).T

    wait_recv(6)
    n_value = sum_of(m_recv)
    n_send[...] = n_value
    start(7)
    n_recv[me["dp"]] = n_value

    wait_recv(5)
    back_all = bg_recv[...].reshape(every, width)
    right = jnp.concatenate([back_all, -times_i(back_all)], axis=1)
    right_high = right.astype(jnp.bfloat16)
    right_low = (right - right_high.astype(jnp.float32)).astype(jnp.bfloat16)
    grad = dot(left, right_high) + dot(left, right_low)
    for k3 in range(MZ):
        for part_index in range(2):
            out_spec[k3, part_index] = grad[
                k3 * width : (k3 + 1) * width, part_index * width : (part_index + 1) * width
            ]

    wait_recv(7)
    out_local[...] = n_recv[...].reshape(width, width)
    for phase in exchanges:
        wait_send(phase)
    for one in shares:
        one.wait_send()


def copy_out(spec_in, local_in, out_spec, out_local):
    out_spec[...] = spec_in[...]
    out_local[...] = local_in[...]


def body(fields, targets, lists, counts, spectral_w, local_w, proj):
    _, slots, planes, length, _, width = fields.shape
    cells = length * length
    work, near = slots - SHARED, slots - 2 * SHARED
    xphase, fwd_table, inv_table = tables(length)
    vmem = pl.BlockSpec(memory_space=pltpu.VMEM)
    f32, bf16 = jnp.float32, jnp.bfloat16
    results = (
        jax.ShapeDtypeStruct(spectral_w.shape, f32),
        jax.ShapeDtypeStruct(local_w.shape, f32),
    )
    fixed = (
        jnp.asarray(fwd_table), jnp.asarray(xphase), lists, counts, targets.reshape(slots, planes, cells),
        jnp.asarray(inv_table), local_w, proj.reshape(1, width), spectral_w,
    )
    in_smem = (1, 2, 3)
    eight = pltpu.VMEM((N_DEV, 8, width), f32)
    sixteen = pltpu.VMEM((N_DEV, 4 * (slots - near), width), f32)
    hbm = pl.BlockSpec(memory_space=pltpu.HBM)
    grads = pl.pallas_call(
        functools.partial(kernel, length, slots, planes),
        out_shape=tuple(pltpu.VMEM(r.shape, r.dtype) for r in results),
        in_specs=[hbm] * (1 + INPUTS),
        out_specs=(vmem, vmem),
        scratch_shapes=[
            *((pltpu.SMEM if index in in_smem else pltpu.VMEM)(a.shape, a.dtype) for index, a in enumerate(fixed)),
            pltpu.VMEM((slots, planes, cells, width), bf16),
            pltpu.VMEM((slots, planes, cells, width), bf16),
            pltpu.VMEM((SHARED, planes, cells, width), bf16),
            pltpu.VMEM((cells // PART, PART, width), bf16),
            pltpu.VMEM((cells, width), bf16),
            pltpu.VMEM((2 * width, 2 * width), bf16),
            pltpu.VMEM((slots * planes, ROWS, width), f32),
            pltpu.VMEM((SHARED * planes, ROWS, width), f32),
            pltpu.VMEM((16, cells), f32), pltpu.VMEM((8, cells), f32), pltpu.VMEM((8, cells), f32),
            pltpu.VMEM((slots, MX, ROWS, width), f32),
            pltpu.VMEM((N_DEV, width // N_DEV, width), f32),
            eight, eight, sixteen, sixteen,
            pltpu.VMEM((8, width), bf16), pltpu.VMEM((N_DEV, 8, width), bf16),
            pltpu.VMEM((16, width), bf16), pltpu.VMEM((N_DEV, 16, width), bf16),
            pltpu.VMEM((4 * slots, width), f32), pltpu.VMEM((N_DEV, 4 * slots, width), f32),
            eight, eight, eight, eight,
            pltpu.VMEM((4 * work, width), f32), pltpu.VMEM((N_DEV, 4 * work, width), f32),
            eight,
            pltpu.VMEM((8, width), f32), eight,
            pltpu.VMEM((8, width), f32), eight,
            pltpu.SemaphoreType.DMA((slots + INPUTS,)),
            pltpu.SemaphoreType.DMA((11,)),
            pltpu.SemaphoreType.DMA((11,)),
            pltpu.SemaphoreType.DMA((3,)),
            pltpu.SemaphoreType.DMA((3,)),
        ],
        compiler_params=pltpu.CompilerParams(
            collective_id=0, has_side_effects=True, vmem_limit_bytes=48 * 1024 * 1024
        ),
        name="fno_step",
    )(*(pltpu.with_memory_space_constraint(a, pltpu.HBM) for a in (fields.reshape(slots, planes, cells, width), *fixed)))
    return pl.pallas_call(
        copy_out, out_shape=results, in_specs=[vmem, vmem], out_specs=(vmem, vmem), name="copy_out",
        compiler_params=pltpu.CompilerParams(vmem_limit_bytes=2 * 1024 * 1024),
    )(*grads)


def solution(mesh):
    return jax.shard_map(
        body,
        mesh=mesh,
        in_specs=(
            P("dp", None, "fsdp", None, None, None),
            P("dp", None, "fsdp", None),
            P("dp", None),
            P(),
            P("fsdp", None, None, None),
            P(),
            P(),
        ),
        out_specs=(P("fsdp", None, None, None), P()),
        check_vma=False,
    )
```

```python
import functools
import math

import jax
import jax.numpy as jnp
import numpy as np
from jax import lax
from jax.experimental import pallas as pl
from jax.experimental.pallas import tpu as pltpu
from jax.sharding import PartitionSpec as P

MX, MY, MZ = 4, 4, 2
N_DEV = 16
ROWS = MY * MZ * 2
ROOT_HALF = 0.7071067811865476
INV_ROOT_TWO_PI = 0.3989422804014327
LOG2_E = 1.4426950408889634
MESH = pl.DeviceIdType.MESH
PART = 1152
UNROLL = 3
INPUTS = 9
SHARED = 2


def phases(ids, length):
    product = (ids[:, None] * np.arange(length)[None, :]) % length
    angle = product.astype(np.float32) * np.float32(2.0 * math.pi / length)
    return np.cos(angle).astype(np.float32), np.sin(angle).astype(np.float32)


def split_bf16(values):
    high = values.astype(jnp.bfloat16)
    low = (values - high.astype(np.float32)).astype(jnp.bfloat16)
    return high, low


@functools.lru_cache(maxsize=None)
def tables(length):
    cos_x, sin_x = phases(np.arange(MX) - MX // 2, length)
    cos_y, sin_y = phases(np.arange(MY) - MY // 2, length)
    cos_z, sin_z = phases(np.arange(MZ), length)
    round_z = lambda t: t.astype(jnp.bfloat16).astype(np.float32)

    def product(cz, sz):
        re = cos_y[:, None, :, None] * cz[None, :, None, :] - sin_y[:, None, :, None] * sz[None, :, None, :]
        im = sin_y[:, None, :, None] * cz[None, :, None, :] + cos_y[:, None, :, None] * sz[None, :, None, :]
        shape = (MY, MZ, length * length)
        return re.reshape(shape), -im.reshape(shape)

    re, im = product(round_z(cos_z), round_z(sin_z))
    forward = np.concatenate(split_bf16(np.stack([re, im], axis=2).reshape(ROWS, -1)), axis=0)
    re, im = product(cos_z, sin_z)
    back = np.stack([re, im], axis=2).reshape(ROWS, -1) * np.float32(float(MX * MY * MZ) ** -0.5)
    high, low = split_bf16(back)
    inverse = np.concatenate([high, low, high], axis=0)
    return np.stack([cos_x, sin_x]).reshape(2, -1), forward, inverse


def times_i(values):
    rows, width = values.shape
    grouped = values.reshape(rows // 8, 8, width)
    even = lax.broadcasted_iota(jnp.int32, grouped.shape, 1) % 2 == 0
    turned = jnp.where(even, -pltpu.roll(grouped, 7, 1), pltpu.roll(grouped, 1, 1))
    return turned.reshape(rows, width)


def dot(a, b):
    return jnp.dot(a, b, preferred_element_type=jnp.float32)


def kernel(
    length, slots, planes,
    fields, *rest,
):
    inputs, (out_spec, out_local), rest = rest[:INPUTS], rest[INPUTS : INPUTS + 2], rest[INPUTS + 2 :]
    kept, rest = rest[:INPUTS], rest[INPUTS:]
    fwd_table, xphase, lists, counts, targets, inv_table, local_w, proj, spec_w = kept
    (
    fbuf, pbuf, f_share, d_buf, cell_table, rhs, inv_rows, inv_share, tgt, tgt_send, tgt_share, acc, local_acc,
    ca_send, ca_recv, cb_send, cb_recv, sa_send, sa_recv, sb_send, sb_recv, cg_send, cg_recv,
    ba_send, ba_recv, bb_send, bb_recv, bg_send, bg_recv,
    l_recv, m_send, m_recv, n_send, n_recv,
    load_sem, send_sem, recv_sem, share_send_sem, share_recv_sem,
    ) = rest
    cells = length * length
    width = fields.shape[-1]
    near = slots - 2 * SHARED
    work = slots - SHARED
    units = work * planes
    half = units // 2
    parts = cells // PART
    me = {"fsdp": lax.axis_index("fsdp"), "dp": lax.axis_index("dp")}
    partner = me["dp"] + 1 - 2 * lax.rem(me["dp"], 2)
    offsets = [8 + ((t + 1) // 2) * (1 - 2 * (t % 2)) for t in range(N_DEV - 1)]

    def peer_of(axis, t):
        return lax.rem(me[axis] + offsets[t], N_DEV)

    exchanges = {
        0: ("fsdp", lambda peer: ca_send.at[peer], ca_recv),
        1: ("fsdp", lambda peer: sa_send, sa_recv),
        2: ("dp", lambda peer: cg_send, cg_recv),
        3: ("fsdp", lambda peer: ba_send.at[peer], ba_recv),
        4: ("dp", lambda peer: local_acc.at[peer], l_recv),
        5: ("dp", lambda peer: bg_send, bg_recv),
        6: ("fsdp", lambda peer: m_send, m_recv),
        7: ("dp", lambda peer: n_send, n_recv),
        8: ("fsdp", lambda peer: cb_send.at[peer], cb_recv),
        9: ("fsdp", lambda peer: sb_send, sb_recv),
        10: ("fsdp", lambda peer: bb_send.at[peer], bb_recv),
    }

    def start(phase):
        axis, src, landing = exchanges[phase]
        for t in range(N_DEV - 1):
            peer = peer_of(axis, t)
            pltpu.make_async_remote_copy(
                src_ref=src(peer), dst_ref=landing.at[me[axis]],
                send_sem=send_sem.at[phase], recv_sem=recv_sem.at[phase],
                device_id={axis: peer}, device_id_type=MESH,
            ).start()

    def all_of(phase):
        axis, _, landing = exchanges[phase]
        bytes_of_all = landing.at[pl.ds(0, N_DEV - 1)]
        return pltpu.make_async_remote_copy(
            src_ref=bytes_of_all, dst_ref=bytes_of_all,
            send_sem=send_sem.at[phase], recv_sem=recv_sem.at[phase],
            device_id={axis: peer_of(axis, 0)}, device_id_type=MESH,
        )

    wait_recv = lambda phase: all_of(phase).wait_recv()
    wait_send = lambda phase: all_of(phase).wait_send()

    def share(index, src, dst):
        return pltpu.make_async_remote_copy(
            src_ref=src, dst_ref=dst,
            send_sem=share_send_sem.at[index], recv_sem=share_recv_sem.at[index],
            device_id={"dp": partner}, device_id_type=MESH,
        )

    shares = [
        share(0, tgt_send, tgt_share),
        share(1, pbuf.at[pl.ds(work, SHARED)], f_share),
        share(2, inv_rows.at[pl.ds(units, SHARED * planes)], inv_share),
    ]

    def load(slot):
        return pltpu.make_async_copy(fields.at[slot], fbuf.at[slot], load_sem.at[slot])

    fetches = [
        pltpu.make_async_copy(src, dst, load_sem.at[slots + index]) for index, (src, dst) in enumerate(zip(inputs, kept))
    ]
    for fetch in fetches[:4]:
        fetch.start()
    for slot in range(slots):
        load(slot).start()
    for fetch in fetches[4:]:
        fetch.start()

    barrier = pltpu.get_barrier_semaphore()
    for axis in ("fsdp", "dp"):
        for t in range(N_DEV - 1):
            pl.semaphore_signal(barrier, inc=1, device_id={axis: peer_of(axis, t)}, device_id_type=MESH)

    def x_phase(part_index, k1, plane):
        return xphase[part_index, k1 * length + me["fsdp"] * planes + plane]

    def fold_modes(slot, plane, product):
        direct = product[0:ROWS] + product[ROWS : 2 * ROWS]
        turned = times_i(direct)
        for k1 in range(MX):
            acc[slot, k1] += x_phase(0, k1, plane) * direct - x_phase(1, k1, plane) * turned

    def pack_modes(send, picks):
        for k1 in range(MX):
            for k2 in range(MY):
                send[k1 * MY + k2] = jnp.concatenate([acc[p, k1, 4 * k2 : 4 * k2 + 4] for p in picks], axis=0)

    acc[...] = jnp.zeros_like(acc)
    for fetch in fetches[:4]:
        fetch.wait()
    order = [lists[0, j] for j in range(slots)]
    my_count, partner_count = counts[me["dp"]], counts[partner]
    mine = my_count > 2
    shared_live = jnp.maximum(my_count, partner_count) > 2

    for slot in range(slots):
        load(slot).wait()

        def forward_plane(plane, carry, slot=slot):
            fold_modes(slot, plane, dot(fwd_table[...], fbuf[slot, plane]))
            return carry

        lax.fori_loop(0, planes, forward_plane, 0)
    pack_modes(ca_send, order[:near])
    pl.semaphore_wait(barrier, 2 * (N_DEV - 1))
    start(0)
    pack_modes(cb_send, order[near:])

    for fetch in fetches[4:]:
        fetch.wait()
    tgt[...] = jnp.zeros_like(tgt)
    tgt_send[...] = jnp.zeros_like(tgt_send)
    for j in range(SHARED):
        tgt_send[planes * j : planes * (j + 1)] = targets[order[work + j]].astype(jnp.float32)
    shares[0].start()

    def by_position(j):
        def one(plane, carry):
            pbuf[j, plane] = fbuf[order[j], plane]
            return carry

        lax.fori_loop(0, planes, one, 0)

    for j in range(work, slots):
        by_position(j)
    shares[1].start()
    ca_recv[me["fsdp"]] = ca_send[me["fsdp"]]
    cb_recv[me["fsdp"]] = cb_send[me["fsdp"]]
    for j in range(work):
        tgt[planes * j : planes * (j + 1)] = targets[order[j]].astype(jnp.float32)
        by_position(j)
    start(8)
    rhs[...] = jnp.zeros_like(rhs)
    rhs[0:width, 0:width] = local_w[...]
    acc[...] = jnp.zeros_like(acc)
    local_acc[...] = jnp.zeros_like(local_acc)
    d_buf[...] = jnp.zeros_like(d_buf)
    grid_total = counts[0]
    for lane in range(1, N_DEV):
        grid_total = grid_total + counts[lane]
    scale = 1.0 / (jnp.zeros((1, width), jnp.float32) + grid_total.astype(jnp.float32))
    shares[0].wait_recv()
    tgt[half : 2 * half] = jnp.where(mine, tgt[half : 2 * half], tgt_share[0:half])
    cell_rows = jnp.concatenate(
        [inv_table[...], tgt[...].astype(jnp.bfloat16), jnp.zeros((width - 3 * ROWS - 16, cells), jnp.bfloat16)], axis=0
    )
    cell_table[...] = cell_rows.T

    def sum_of(ref):
        value = ref[0]
        for peer in range(1, N_DEV):
            value = value + ref[peer]
        return value

    def mix(landing, send):
        coeff = (sum_of(landing) * float(length) ** -1.5).astype(jnp.bfloat16)
        coeff_f = coeff.astype(jnp.float32)
        turned = times_i(coeff_f).astype(jnp.bfloat16)
        third = (lax.broadcasted_iota(jnp.int32, coeff.shape, 0) // 2) % 2
        mixed = [dot(coeff, spec_w[k3, 0]) + dot(turned, spec_w[k3, 1]) for k3 in range(MZ)]
        send[...] = jnp.where(third == 0, mixed[0], mixed[1]).astype(jnp.bfloat16)
        return coeff_f

    wait_recv(0)
    coeff_near = mix(ca_recv, sa_send)
    start(1)
    wait_recv(8)
    coeff_far = mix(cb_recv, sb_send)
    start(9)
    cg_send[...] = jnp.concatenate([coeff_near, coeff_far], axis=0)
    sa_recv[me["fsdp"]] = sa_send[...]
    sb_recv[me["fsdp"]] = sb_send[...]
    cg_recv[me["dp"]] = cg_send[...]

    def inverse_rows(landing, first, last):
        for k1 in range(MX):
            owners = [landing[k1 * MY + k2].astype(jnp.float32) for k2 in range(MY)]
            for j in range(last - first):
                piece = jnp.concatenate([o[4 * j : 4 * j + 4] for o in owners], axis=0)
                turned_piece = times_i(piece)
                for plane in range(planes):
                    term = x_phase(0, k1, plane) * piece + x_phase(1, k1, plane) * turned_piece
                    unit = (first + j) * planes + plane
                    if k1 == 0:
                        inv_rows[unit] = term
                    else:
                        inv_rows[unit] += term

    wait_recv(1)
    inverse_rows(sa_recv, 0, near)

    picks = lax.broadcasted_iota(jnp.int32, (width, width), 0)

    def reduce_part(unit, part_index):
        slot, plane = unit // planes, unit % planes
        rows_here = pl.ds(part_index * PART, PART)
        left = jnp.concatenate([pbuf[slot, plane, rows_here].T, fwd_table[:, rows_here]], axis=0)
        product = dot(left, d_buf[part_index])
        local_acc[...] += product[0:width].reshape(local_acc.shape)
        fold_modes(slot, plane, product[width:])

    def point(unit):
        slot, plane = unit // planes, unit % planes
        live = jnp.where(slot < near, jnp.where(slot < my_count, 1, 0), jnp.where(shared_live, 1, 0))
        weight = proj[...] * scale * live.astype(jnp.float32)
        half_proj, half_weight, bell_weight = 0.5 * proj[...], 0.5 * weight, INV_ROOT_TWO_PI * weight
        values = inv_rows[unit]
        high = values.astype(jnp.bfloat16)
        low = (values - high.astype(jnp.float32)).astype(jnp.bfloat16)
        rhs[width : width + 3 * ROWS, 0:width] = jnp.concatenate([high, high, low], axis=0)
        rhs[width : 2 * width, width : 2 * width] = jnp.where(picks == 3 * ROWS + unit, 1.0, 0.0).astype(jnp.bfloat16)
        for part_index in range(parts):
            rows_here = pl.ds(part_index * PART, PART)
            left = jnp.concatenate([pbuf[slot, plane, rows_here], cell_table[rows_here]], axis=1)
            both = dot(left, rhs[...])
            pre, target = both[:, 0:width], both[:, width : 2 * width]
            gate = lax.erf(pre * ROOT_HALF) + 1.0
            bell = jnp.exp2(pre * pre * (-0.5 * LOG2_E))
            pred = jnp.sum(pre * gate * half_proj, axis=1, keepdims=True)
            slope = gate * half_weight + pre * bell * bell_weight
            d_buf[part_index] = ((pred - target) * slope).astype(jnp.bfloat16)
            if part_index == 0:
                reduce_part(jnp.maximum(unit - 1, 0), parts - 1)
            else:
                reduce_part(unit, part_index - 1)

    def step(index, carry):
        first = index * UNROLL

        @pl.when(first == planes)
        def _():
            wait_recv(9)
            inverse_rows(sb_recv, near, slots)
            shares[2].start()
            start(2)

        @pl.when(first == half)
        def _():
            shares[1].wait_recv()
            shares[2].wait_recv()
            inv_rows[half:units] = jnp.where(mine, inv_rows[half:units], inv_share[0:half])

            def one(k, carry):
                slot, plane = k // planes, k % planes
                pbuf[near + slot, plane] = jnp.where(mine, pbuf[near + slot, plane], f_share[slot, plane])
                return carry

            lax.fori_loop(0, half, one, 0)

        @pl.when(first == half + planes)
        def _():
            pack_modes(ba_send, range(near))
            start(3)
            ba_recv[me["fsdp"]] = ba_send[me["fsdp"]]

        for sub in range(UNROLL):
            point(first + sub)
        return carry

    lax.fori_loop(0, units // UNROLL, step, 0)
    reduce_part(units - 1, parts - 1)

    start(4)
    pack_modes(bb_send, range(near, work))
    start(10)
    l_recv[me["dp"]] = local_acc[me["dp"]]
    bb_recv[me["fsdp"]] = bb_send[me["fsdp"]]
    back_scale = float(MX * MY * MZ) ** -0.5
    wait_recv(3)
    near_value = sum_of(ba_recv) * back_scale

    wait_recv(4)
    m_value = sum_of(l_recv)
    m_send[...] = m_value
    start(6)
    m_recv[me["fsdp"]] = m_value
    wait_recv(10)
    bg_send[...] = jnp.concatenate([near_value, sum_of(bb_recv) * back_scale], axis=0)
    start(5)
    bg_recv[me["dp"]] = bg_send[...]

    wait_recv(2)
    first, far = 4 * near, 4 * work
    pieces = []
    for lane in range(N_DEV):
        taken = jnp.where(counts[lane] > 2, cg_recv[lane, first:far], cg_recv[lane ^ 1, far : 4 * slots])
        pieces += [cg_recv[lane, 0:first], taken]
    coeff_all = jnp.concatenate(pieces, axis=0)
    every = N_DEV * far
    third = (lax.broadcasted_iota(jnp.int32, (every, width), 0) // 2) % 2
    left = jnp.concatenate([jnp.where(third == k3, coeff_all, 0.0) for k3 in range(MZ)], axis=1)
    left = left.astype(jnp.bfloat16).T

    wait_recv(6)
    n_value = sum_of(m_recv)
    n_send[...] = n_value
    start(7)
    n_recv[me["dp"]] = n_value

    wait_recv(5)
    back_all = bg_recv[...].reshape(every, width)
    right = jnp.concatenate([back_all, -times_i(back_all)], axis=1)
    right_high = right.astype(jnp.bfloat16)
    right_low = (right - right_high.astype(jnp.float32)).astype(jnp.bfloat16)
    grad = dot(left, right_high) + dot(left, right_low)
    for k3 in range(MZ):
        for part_index in range(2):
            out_spec[k3, part_index] = grad[
                k3 * width : (k3 + 1) * width, part_index * width : (part_index + 1) * width
            ]

    wait_recv(7)
    out_local[...] = n_recv[...].reshape(width, width)
    for phase in exchanges:
        wait_send(phase)
    for one in shares:
        one.wait_send()


def copy_out(spec_in, local_in, out_spec, out_local):
    out_spec[...] = spec_in[...]
    out_local[...] = local_in[...]


def body(fields, targets, lists, counts, spectral_w, local_w, proj):
    _, slots, planes, length, _, width = fields.shape
    cells = length * length
    work, near = slots - SHARED, slots - 2 * SHARED
    xphase, fwd_table, inv_table = tables(length)
    vmem = pl.BlockSpec(memory_space=pltpu.VMEM)
    f32, bf16 = jnp.float32, jnp.bfloat16
    results = (
        jax.ShapeDtypeStruct(spectral_w.shape, f32),
        jax.ShapeDtypeStruct(local_w.shape, f32),
    )
    fixed = (
        jnp.asarray(fwd_table), jnp.asarray(xphase), lists, counts, targets.reshape(slots, planes, cells),
        jnp.asarray(inv_table), local_w, proj.reshape(1, width), spectral_w,
    )
    in_smem = (1, 2, 3)
    eight = pltpu.VMEM((N_DEV, 8, width), f32)
    sixteen = pltpu.VMEM((N_DEV, 4 * (slots - near), width), f32)
    hbm = pl.BlockSpec(memory_space=pltpu.HBM)
    grads = pl.pallas_call(
        functools.partial(kernel, length, slots, planes),
        out_shape=tuple(pltpu.VMEM(r.shape, r.dtype) for r in results),
        in_specs=[hbm] * (1 + INPUTS),
        out_specs=(vmem, vmem),
        scratch_shapes=[
            *((pltpu.SMEM if index in in_smem else pltpu.VMEM)(a.shape, a.dtype) for index, a in enumerate(fixed)),
            pltpu.VMEM((slots, planes, cells, width), bf16),
            pltpu.VMEM((slots, planes, cells, width), bf16),
            pltpu.VMEM((SHARED, planes, cells, width), bf16),
            pltpu.VMEM((cells // PART, PART, width), bf16),
            pltpu.VMEM((cells, width), bf16),
            pltpu.VMEM((2 * width, 2 * width), bf16),
            pltpu.VMEM((slots * planes, ROWS, width), f32),
            pltpu.VMEM((SHARED * planes, ROWS, width), f32),
            pltpu.VMEM((16, cells), f32), pltpu.VMEM((8, cells), f32), pltpu.VMEM((8, cells), f32),
            pltpu.VMEM((slots, MX, ROWS, width), f32),
            pltpu.VMEM((N_DEV, width // N_DEV, width), f32),
            eight, eight, sixteen, sixteen,
            pltpu.VMEM((8, width), bf16), pltpu.VMEM((N_DEV, 8, width), bf16),
            pltpu.VMEM((16, width), bf16), pltpu.VMEM((N_DEV, 16, width), bf16),
            pltpu.VMEM((4 * slots, width), f32), pltpu.VMEM((N_DEV, 4 * slots, width), f32),
            eight, eight, eight, eight,
            pltpu.VMEM((4 * work, width), f32), pltpu.VMEM((N_DEV, 4 * work, width), f32),
            eight,
            pltpu.VMEM((8, width), f32), eight,
            pltpu.VMEM((8, width), f32), eight,
            pltpu.SemaphoreType.DMA((slots + INPUTS,)),
            pltpu.SemaphoreType.DMA((11,)),
            pltpu.SemaphoreType.DMA((11,)),
            pltpu.SemaphoreType.DMA((3,)),
            pltpu.SemaphoreType.DMA((3,)),
        ],
        compiler_params=pltpu.CompilerParams(
            collective_id=0, has_side_effects=True, vmem_limit_bytes=48 * 1024 * 1024,
        ),
        name="fno_step",
    )(*(pltpu.with_memory_space_constraint(a, pltpu.HBM) for a in (fields.reshape(slots, planes, cells, width), *fixed)))
    return pl.pallas_call(
        copy_out, out_shape=results, in_specs=[vmem, vmem], out_specs=(vmem, vmem), name="copy_out",
        compiler_params=pltpu.CompilerParams(vmem_limit_bytes=2 * 1024 * 1024),
    )(*grads)


def solution(mesh):
    return jax.shard_map(
        body,
        mesh=mesh,
        in_specs=(
            P("dp", None, "fsdp", None, None, None),
            P("dp", None, "fsdp", None),
            P("dp", None),
            P(),
            P("fsdp", None, None, None),
            P(),
            P(),
        ),
        out_specs=(P("fsdp", None, None, None), P()),
        check_vma=False,
    )
```

```python
import functools
import math

import jax
import jax.numpy as jnp
import numpy as np
from jax import lax
from jax.experimental import pallas as pl
from jax.experimental.pallas import tpu as pltpu
from jax.sharding import PartitionSpec as P

MX, MY, MZ = 4, 4, 2
N_DEV = 16
ROWS = MY * MZ * 2
ROOT_HALF = 0.7071067811865476
INV_ROOT_TWO_PI = 0.3989422804014327
LOG2_E = 1.4426950408889634
MESH = pl.DeviceIdType.MESH
PART = 1152
UNROLL = 3
INPUTS = 9
SHARED = 2


def phases(ids, length):
    product = (ids[:, None] * np.arange(length)[None, :]) % length
    angle = product.astype(np.float32) * np.float32(2.0 * math.pi / length)
    return np.cos(angle).astype(np.float32), np.sin(angle).astype(np.float32)


def split_bf16(values):
    high = values.astype(jnp.bfloat16)
    low = (values - high.astype(np.float32)).astype(jnp.bfloat16)
    return high, low


@functools.lru_cache(maxsize=None)
def tables(length):
    cos_x, sin_x = phases(np.arange(MX) - MX // 2, length)
    cos_y, sin_y = phases(np.arange(MY) - MY // 2, length)
    cos_z, sin_z = phases(np.arange(MZ), length)
    round_z = lambda t: t.astype(jnp.bfloat16).astype(np.float32)

    def product(cz, sz):
        re = cos_y[:, None, :, None] * cz[None, :, None, :] - sin_y[:, None, :, None] * sz[None, :, None, :]
        im = sin_y[:, None, :, None] * cz[None, :, None, :] + cos_y[:, None, :, None] * sz[None, :, None, :]
        shape = (MY, MZ, length * length)
        return re.reshape(shape), -im.reshape(shape)

    re, im = product(round_z(cos_z), round_z(sin_z))
    forward = np.concatenate(split_bf16(np.stack([re, im], axis=2).reshape(ROWS, -1)), axis=0)
    re, im = product(cos_z, sin_z)
    back = np.stack([re, im], axis=2).reshape(ROWS, -1) * np.float32(float(MX * MY * MZ) ** -0.5)
    high, low = split_bf16(back)
    inverse = np.concatenate([high, low, high], axis=0)
    return np.stack([cos_x, sin_x]).reshape(2, -1), forward, inverse


def times_i(values):
    rows, width = values.shape
    grouped = values.reshape(rows // 8, 8, width)
    even = lax.broadcasted_iota(jnp.int32, grouped.shape, 1) % 2 == 0
    turned = jnp.where(even, -pltpu.roll(grouped, 7, 1), pltpu.roll(grouped, 1, 1))
    return turned.reshape(rows, width)


def dot(a, b):
    return jnp.dot(a, b, preferred_element_type=jnp.float32)


def kernel(
    length, slots, planes,
    fields, *rest,
):
    inputs, (out_spec, out_local), rest = rest[:INPUTS], rest[INPUTS : INPUTS + 2], rest[INPUTS + 2 :]
    kept, rest = rest[:INPUTS], rest[INPUTS:]
    fwd_table, xphase, lists, counts, targets, inv_table, local_w, proj, spec_w = kept
    (
    fbuf, pbuf, p_turned, f_share, d_buf, cell_table, rhs, inv_rows, inv_share, tgt, tgt_send, tgt_share, acc, local_acc,
    ca_send, ca_recv, cb_send, cb_recv, sa_send, sa_recv, sb_send, sb_recv, cg_send, cg_recv,
    ba_send, ba_recv, bb_send, bb_recv, bg_send, bg_recv,
    l_recv, m_send, m_recv, n_send, n_recv,
    load_sem, send_sem, recv_sem, share_send_sem, share_recv_sem,
    ) = rest
    cells = length * length
    width = fields.shape[-1]
    near = slots - 2 * SHARED
    work = slots - SHARED
    units = work * planes
    half = units // 2
    parts = cells // PART
    me = {"fsdp": lax.axis_index("fsdp"), "dp": lax.axis_index("dp")}
    partner = me["dp"] + 1 - 2 * lax.rem(me["dp"], 2)
    offsets = [8 + ((t + 1) // 2) * (1 - 2 * (t % 2)) for t in range(N_DEV - 1)]

    def peer_of(axis, t):
        return lax.rem(me[axis] + offsets[t], N_DEV)

    exchanges = {
        0: ("fsdp", lambda peer: ca_send.at[peer], ca_recv),
        1: ("fsdp", lambda peer: sa_send, sa_recv),
        2: ("dp", lambda peer: cg_send, cg_recv),
        3: ("fsdp", lambda peer: ba_send.at[peer], ba_recv),
        4: ("dp", lambda peer: local_acc.at[peer], l_recv),
        5: ("dp", lambda peer: bg_send, bg_recv),
        6: ("fsdp", lambda peer: m_send, m_recv),
        7: ("dp", lambda peer: n_send, n_recv),
        8: ("fsdp", lambda peer: cb_send.at[peer], cb_recv),
        9: ("fsdp", lambda peer: sb_send, sb_recv),
        10: ("fsdp", lambda peer: bb_send.at[peer], bb_recv),
    }

    def start(phase):
        axis, src, landing = exchanges[phase]
        for t in range(N_DEV - 1):
            peer = peer_of(axis, t)
            pltpu.make_async_remote_copy(
                src_ref=src(peer), dst_ref=landing.at[me[axis]],
                send_sem=send_sem.at[phase], recv_sem=recv_sem.at[phase],
                device_id={axis: peer}, device_id_type=MESH,
            ).start()

    def all_of(phase):
        axis, _, landing = exchanges[phase]
        bytes_of_all = landing.at[pl.ds(0, N_DEV - 1)]
        return pltpu.make_async_remote_copy(
            src_ref=bytes_of_all, dst_ref=bytes_of_all,
            send_sem=send_sem.at[phase], recv_sem=recv_sem.at[phase],
            device_id={axis: peer_of(axis, 0)}, device_id_type=MESH,
        )

    wait_recv = lambda phase: all_of(phase).wait_recv()
    wait_send = lambda phase: all_of(phase).wait_send()

    def share(index, src, dst):
        return pltpu.make_async_remote_copy(
            src_ref=src, dst_ref=dst,
            send_sem=share_send_sem.at[index], recv_sem=share_recv_sem.at[index],
            device_id={"dp": partner}, device_id_type=MESH,
        )

    shares = [
        share(0, tgt_send, tgt_share),
        share(1, pbuf.at[pl.ds(work, SHARED)], f_share),
        share(2, inv_rows.at[pl.ds(units, SHARED * planes)], inv_share),
    ]

    def load(slot):
        return pltpu.make_async_copy(fields.at[slot], fbuf.at[slot], load_sem.at[slot])

    fetches = [
        pltpu.make_async_copy(src, dst, load_sem.at[slots + index]) for index, (src, dst) in enumerate(zip(inputs, kept))
    ]
    for fetch in fetches[:4]:
        fetch.start()
    for slot in range(slots):
        load(slot).start()
    for fetch in fetches[4:]:
        fetch.start()

    barrier = pltpu.get_barrier_semaphore()
    for axis in ("fsdp", "dp"):
        for t in range(N_DEV - 1):
            pl.semaphore_signal(barrier, inc=1, device_id={axis: peer_of(axis, t)}, device_id_type=MESH)

    def x_phase(part_index, k1, plane):
        return xphase[part_index, k1 * length + me["fsdp"] * planes + plane]

    def fold_modes(slot, plane, product):
        direct = product[0:ROWS] + product[ROWS : 2 * ROWS]
        turned = times_i(direct)
        for k1 in range(MX):
            acc[slot, k1] += x_phase(0, k1, plane) * direct - x_phase(1, k1, plane) * turned

    def pack_modes(send, picks):
        for k1 in range(MX):
            for k2 in range(MY):
                send[k1 * MY + k2] = jnp.concatenate([acc[p, k1, 4 * k2 : 4 * k2 + 4] for p in picks], axis=0)

    acc[...] = jnp.zeros_like(acc)
    for fetch in fetches[:4]:
        fetch.wait()
    order = [lists[0, j] for j in range(slots)]
    my_count, partner_count = counts[me["dp"]], counts[partner]
    mine = my_count > 2
    shared_live = jnp.maximum(my_count, partner_count) > 2

    for slot in range(slots):
        load(slot).wait()

        for plane in range(planes):
            fold_modes(slot, plane, dot(fwd_table[...], fbuf[slot, plane]))
    pack_modes(ca_send, order[:near])
    pl.semaphore_wait(barrier, 2 * (N_DEV - 1))
    start(0)
    pack_modes(cb_send, order[near:])

    for fetch in fetches[4:]:
        fetch.wait()
    tgt[...] = jnp.zeros_like(tgt)
    tgt_send[...] = jnp.zeros_like(tgt_send)
    for j in range(SHARED):
        tgt_send[planes * j : planes * (j + 1)] = targets[order[work + j]].astype(jnp.float32)
    shares[0].start()

    def by_position(j):
        def one(plane, carry):
            value = fbuf[order[j], plane]
            pbuf[j, plane] = value
            if j < near:
                p_turned[j, plane] = value.T
            return carry

        lax.fori_loop(0, planes, one, 0)

    for j in range(work, slots):
        by_position(j)
    shares[1].start()
    ca_recv[me["fsdp"]] = ca_send[me["fsdp"]]
    cb_recv[me["fsdp"]] = cb_send[me["fsdp"]]
    start(8)
    for j in range(work):
        tgt[planes * j : planes * (j + 1)] = targets[order[j]].astype(jnp.float32)
        by_position(j)
    rhs[...] = jnp.zeros_like(rhs)
    rhs[0:width, 0:width] = local_w[...]
    acc[...] = jnp.zeros_like(acc)
    local_acc[...] = jnp.zeros_like(local_acc)
    d_buf[...] = jnp.zeros_like(d_buf)
    grid_total = counts[0]
    for lane in range(1, N_DEV):
        grid_total = grid_total + counts[lane]
    scale = 1.0 / (jnp.zeros((1, width), jnp.float32) + grid_total.astype(jnp.float32))
    shares[0].wait_recv()
    tgt[half : 2 * half] = jnp.where(mine, tgt[half : 2 * half], tgt_share[0:half])
    cell_rows = jnp.concatenate(
        [inv_table[...], tgt[...].astype(jnp.bfloat16), jnp.zeros((width - 3 * ROWS - 16, cells), jnp.bfloat16)], axis=0
    )
    cell_table[...] = cell_rows.T

    def sum_of(ref):
        value = ref[0]
        for peer in range(1, N_DEV):
            value = value + ref[peer]
        return value

    def mix(landing, send):
        coeff = (sum_of(landing) * float(length) ** -1.5).astype(jnp.bfloat16)
        coeff_f = coeff.astype(jnp.float32)
        turned = times_i(coeff_f).astype(jnp.bfloat16)
        third = (lax.broadcasted_iota(jnp.int32, coeff.shape, 0) // 2) % 2
        mixed = [dot(coeff, spec_w[k3, 0]) + dot(turned, spec_w[k3, 1]) for k3 in range(MZ)]
        send[...] = jnp.where(third == 0, mixed[0], mixed[1]).astype(jnp.bfloat16)
        return coeff_f

    wait_recv(0)
    coeff_near = mix(ca_recv, sa_send)
    start(1)
    wait_recv(8)
    coeff_far = mix(cb_recv, sb_send)
    start(9)
    cg_send[...] = jnp.concatenate([coeff_near, coeff_far], axis=0)
    sa_recv[me["fsdp"]] = sa_send[...]
    sb_recv[me["fsdp"]] = sb_send[...]
    cg_recv[me["dp"]] = cg_send[...]

    def inverse_rows(landing, first, last):
        for k1 in range(MX):
            owners = [landing[k1 * MY + k2].astype(jnp.float32) for k2 in range(MY)]
            for j in range(last - first):
                piece = jnp.concatenate([o[4 * j : 4 * j + 4] for o in owners], axis=0)
                turned_piece = times_i(piece)
                for plane in range(planes):
                    term = x_phase(0, k1, plane) * piece + x_phase(1, k1, plane) * turned_piece
                    unit = (first + j) * planes + plane
                    if k1 == 0:
                        inv_rows[unit] = term
                    else:
                        inv_rows[unit] += term

    shares[1].wait_recv()

    def choose(k, carry):
        slot, plane = near + k // planes, k % planes
        value = jnp.where(mine, pbuf[slot, plane], f_share[k // planes, plane])
        pbuf[slot, plane] = value
        p_turned[slot, plane] = value.T
        return carry

    lax.fori_loop(0, half, choose, 0)
    wait_recv(1)
    inverse_rows(sa_recv, 0, near)

    picks = lax.broadcasted_iota(jnp.int32, (width, width), 0)

    def reduce_part(unit, part_index):
        slot, plane = unit // planes, unit % planes
        rows_here = pl.ds(part_index * PART, PART)
        left = jnp.concatenate([p_turned[slot, plane, :, rows_here], fwd_table[:, rows_here]], axis=0)
        product = dot(left, d_buf[part_index])
        local_acc[...] += product[0:width, 0:width].reshape(local_acc.shape)
        fold_modes(slot, plane, product[width:, 0:width])

    def point(unit):
        slot, plane = unit // planes, unit % planes
        live = jnp.where(slot < near, jnp.where(slot < my_count, 1, 0), jnp.where(shared_live, 1, 0))
        weight = proj[...] * scale * live.astype(jnp.float32)
        half_proj, half_weight, bell_weight = 0.5 * proj[...], 0.5 * weight, INV_ROOT_TWO_PI * weight
        values = inv_rows[unit]
        high = values.astype(jnp.bfloat16)
        low = (values - high.astype(jnp.float32)).astype(jnp.bfloat16)
        rhs[width : width + 3 * ROWS, 0:width] = jnp.concatenate([high, high, low], axis=0)
        rhs[width : 2 * width, width : 2 * width] = jnp.where(picks == 3 * ROWS + unit, 1.0, 0.0).astype(jnp.bfloat16)
        for part_index in range(parts):
            rows_here = pl.ds(part_index * PART, PART)
            left = jnp.concatenate([pbuf[slot, plane, rows_here], cell_table[rows_here]], axis=1)
            both = dot(left, rhs[...])
            pre, target = both[:, 0:width], both[:, width : 2 * width]
            gate = lax.erf(pre * ROOT_HALF) + 1.0
            bell = jnp.exp2(pre * pre * (-0.5 * LOG2_E))
            pred = jnp.sum(pre * gate * half_proj, axis=1, keepdims=True)
            slope = gate * half_weight + pre * bell * bell_weight
            d_buf[part_index, :, 0:width] = ((pred - target) * slope).astype(jnp.bfloat16)
            if part_index == 0:
                reduce_part(jnp.maximum(unit - 1, 0), parts - 1)
            else:
                reduce_part(unit, part_index - 1)

    def step(index, carry):
        first = index * UNROLL

        @pl.when(first == planes)
        def _():
            wait_recv(9)
            inverse_rows(sb_recv, near, slots)
            shares[2].start()
            start(2)

        @pl.when(first == half)
        def _():
            shares[2].wait_recv()
            inv_rows[half:units] = jnp.where(mine, inv_rows[half:units], inv_share[0:half])

        @pl.when(first == half + planes)
        def _():
            pack_modes(ba_send, range(near))
            start(3)
            ba_recv[me["fsdp"]] = ba_send[me["fsdp"]]

        for sub in range(UNROLL):
            point(first + sub)
        return carry

    lax.fori_loop(0, units // UNROLL, step, 0)
    reduce_part(units - 1, parts - 1)

    start(4)
    pack_modes(bb_send, range(near, work))
    start(10)
    l_recv[me["dp"]] = local_acc[me["dp"]]
    bb_recv[me["fsdp"]] = bb_send[me["fsdp"]]
    back_scale = float(MX * MY * MZ) ** -0.5
    wait_recv(3)
    near_value = sum_of(ba_recv) * back_scale

    wait_recv(4)
    m_value = sum_of(l_recv)
    m_send[...] = m_value
    start(6)
    m_recv[me["fsdp"]] = m_value
    wait_recv(10)
    bg_send[...] = jnp.concatenate([near_value, sum_of(bb_recv) * back_scale], axis=0)
    start(5)
    bg_recv[me["dp"]] = bg_send[...]

    wait_recv(2)
    first, far = 4 * near, 4 * work
    pieces = []
    for lane in range(N_DEV):
        taken = jnp.where(counts[lane] > 2, cg_recv[lane, first:far], cg_recv[lane ^ 1, far : 4 * slots])
        pieces += [cg_recv[lane, 0:first], taken]
    coeff_all = jnp.concatenate(pieces, axis=0)
    every = N_DEV * far
    third = (lax.broadcasted_iota(jnp.int32, (every, width), 0) // 2) % 2
    left = jnp.concatenate([jnp.where(third == k3, coeff_all, 0.0) for k3 in range(MZ)], axis=1)
    left = left.astype(jnp.bfloat16).T

    wait_recv(6)
    n_value = sum_of(m_recv)
    n_send[...] = n_value
    start(7)
    n_recv[me["dp"]] = n_value

    wait_recv(5)
    back_all = bg_recv[...].reshape(every, width)
    right = jnp.concatenate([back_all, -times_i(back_all)], axis=1)
    right_high = right.astype(jnp.bfloat16)
    right_low = (right - right_high.astype(jnp.float32)).astype(jnp.bfloat16)
    grad = dot(left, right_high) + dot(left, right_low)
    for k3 in range(MZ):
        for part_index in range(2):
            out_spec[k3, part_index] = grad[
                k3 * width : (k3 + 1) * width, part_index * width : (part_index + 1) * width
            ]

    wait_recv(7)
    out_local[...] = n_recv[...].reshape(width, width)
    for phase in exchanges:
        wait_send(phase)
    for one in shares:
        one.wait_send()


def copy_out(spec_in, local_in, out_spec, out_local, sem):
    copies = [
        pltpu.make_async_copy(src, dst, sem.at[index])
        for index, (src, dst) in enumerate(((spec_in, out_spec), (local_in, out_local)))
    ]
    for copy in copies:
        copy.start()
    for copy in copies:
        copy.wait()


def body(fields, targets, lists, counts, spectral_w, local_w, proj):
    _, slots, planes, length, _, width = fields.shape
    cells = length * length
    work, near = slots - SHARED, slots - 2 * SHARED
    xphase, fwd_table, inv_table = tables(length)
    vmem = pl.BlockSpec(memory_space=pltpu.VMEM)
    f32, bf16 = jnp.float32, jnp.bfloat16
    results = (
        jax.ShapeDtypeStruct(spectral_w.shape, f32),
        jax.ShapeDtypeStruct(local_w.shape, f32),
    )
    fixed = (
        jnp.asarray(fwd_table), jnp.asarray(xphase), lists, counts, targets.reshape(slots, planes, cells),
        jnp.asarray(inv_table), local_w, proj.reshape(1, width), spectral_w,
    )
    in_smem = (1, 2, 3)
    eight = pltpu.VMEM((N_DEV, 8, width), f32)
    sixteen = pltpu.VMEM((N_DEV, 4 * (slots - near), width), f32)
    hbm = pl.BlockSpec(memory_space=pltpu.HBM)
    grads = pl.pallas_call(
        functools.partial(kernel, length, slots, planes),
        out_shape=tuple(pltpu.VMEM(r.shape, r.dtype) for r in results),
        in_specs=[hbm] * (1 + INPUTS),
        out_specs=(vmem, vmem),
        scratch_shapes=[
            *((pltpu.SMEM if index in in_smem else pltpu.VMEM)(a.shape, a.dtype) for index, a in enumerate(fixed)),
            pltpu.VMEM((slots, planes, cells, width), bf16),
            pltpu.VMEM((slots, planes, cells, width), bf16),
            pltpu.VMEM((work, planes, width, cells), bf16),
            pltpu.VMEM((SHARED, planes, cells, width), bf16),
            pltpu.VMEM((cells // PART, PART, 2 * width), bf16),
            pltpu.VMEM((cells, width), bf16),
            pltpu.VMEM((2 * width, 2 * width), bf16),
            pltpu.VMEM((slots * planes, ROWS, width), f32),
            pltpu.VMEM((SHARED * planes, ROWS, width), f32),
            pltpu.VMEM((16, cells), f32), pltpu.VMEM((8, cells), f32), pltpu.VMEM((8, cells), f32),
            pltpu.VMEM((slots, MX, ROWS, width), f32),
            pltpu.VMEM((N_DEV, width // N_DEV, width), f32),
            eight, eight, sixteen, sixteen,
            pltpu.VMEM((8, width), bf16), pltpu.VMEM((N_DEV, 8, width), bf16),
            pltpu.VMEM((16, width), bf16), pltpu.VMEM((N_DEV, 16, width), bf16),
            pltpu.VMEM((4 * slots, width), f32), pltpu.VMEM((N_DEV, 4 * slots, width), f32),
            eight, eight, eight, eight,
            pltpu.VMEM((4 * work, width), f32), pltpu.VMEM((N_DEV, 4 * work, width), f32),
            eight,
            pltpu.VMEM((8, width), f32), eight,
            pltpu.VMEM((8, width), f32), eight,
            pltpu.SemaphoreType.DMA((slots + INPUTS,)),
            pltpu.SemaphoreType.DMA((11,)),
            pltpu.SemaphoreType.DMA((11,)),
            pltpu.SemaphoreType.DMA((3,)),
            pltpu.SemaphoreType.DMA((3,)),
        ],
        compiler_params=pltpu.CompilerParams(
            collective_id=0, has_side_effects=True, vmem_limit_bytes=48 * 1024 * 1024,

        ),
        name="fno_step",
    )(*(pltpu.with_memory_space_constraint(a, pltpu.HBM) for a in (fields.reshape(slots, planes, cells, width), *fixed)))
    return pl.pallas_call(
        copy_out, out_shape=results, in_specs=[vmem, vmem], out_specs=(hbm, hbm), name="copy_out",
        scratch_shapes=[pltpu.SemaphoreType.DMA((2,))],
        compiler_params=pltpu.CompilerParams(vmem_limit_bytes=2 * 1024 * 1024),
    )(*grads)


def solution(mesh):
    return jax.shard_map(
        body,
        mesh=mesh,
        in_specs=(
            P("dp", None, "fsdp", None, None, None),
            P("dp", None, "fsdp", None),
            P("dp", None),
            P(),
            P("fsdp", None, None, None),
            P(),
            P(),
        ),
        out_specs=(P("fsdp", None, None, None), P()),
        check_vma=False,
    )
```

```python
import functools
import math

import jax
import jax.numpy as jnp
import numpy as np
from jax import lax
from jax.experimental import pallas as pl
from jax.experimental.pallas import tpu as pltpu
from jax.sharding import PartitionSpec as P

MX, MY, MZ = 4, 4, 2
N_DEV = 16
ROWS = MY * MZ * 2
ROOT_HALF = 0.7071067811865476
INV_ROOT_TWO_PI = 0.3989422804014327
LOG2_E = 1.4426950408889634
MESH = pl.DeviceIdType.MESH
PART = 1152
UNROLL = 3
INPUTS = 9
SHARED = 2


def phases(ids, length):
    product = (ids[:, None] * np.arange(length)[None, :]) % length
    angle = product.astype(np.float32) * np.float32(2.0 * math.pi / length)
    return np.cos(angle).astype(np.float32), np.sin(angle).astype(np.float32)


def split_bf16(values):
    high = values.astype(jnp.bfloat16)
    low = (values - high.astype(np.float32)).astype(jnp.bfloat16)
    return high, low


@functools.lru_cache(maxsize=None)
def tables(length):
    cos_x, sin_x = phases(np.arange(MX) - MX // 2, length)
    cos_y, sin_y = phases(np.arange(MY) - MY // 2, length)
    cos_z, sin_z = phases(np.arange(MZ), length)
    round_z = lambda t: t.astype(jnp.bfloat16).astype(np.float32)

    def product(cz, sz):
        re = cos_y[:, None, :, None] * cz[None, :, None, :] - sin_y[:, None, :, None] * sz[None, :, None, :]
        im = sin_y[:, None, :, None] * cz[None, :, None, :] + cos_y[:, None, :, None] * sz[None, :, None, :]
        shape = (MY, MZ, length * length)
        return re.reshape(shape), -im.reshape(shape)

    re, im = product(round_z(cos_z), round_z(sin_z))
    forward = np.concatenate(split_bf16(np.stack([re, im], axis=2).reshape(ROWS, -1)), axis=0)
    re, im = product(cos_z, sin_z)
    back = np.stack([re, im], axis=2).reshape(ROWS, -1) * np.float32(float(MX * MY * MZ) ** -0.5)
    high, low = split_bf16(back)
    inverse = np.concatenate([high, low, high], axis=0)
    return np.stack([cos_x, sin_x]).reshape(2, -1), forward, inverse


def times_i(values):
    rows, width = values.shape
    grouped = values.reshape(rows // 8, 8, width)
    even = lax.broadcasted_iota(jnp.int32, grouped.shape, 1) % 2 == 0
    turned = jnp.where(even, -pltpu.roll(grouped, 7, 1), pltpu.roll(grouped, 1, 1))
    return turned.reshape(rows, width)


def dot(a, b):
    return jnp.dot(a, b, preferred_element_type=jnp.float32)


def kernel(
    length, slots, planes,
    fields, *rest,
):
    inputs, (out_spec, out_local), rest = rest[:INPUTS], rest[INPUTS : INPUTS + 2], rest[INPUTS + 2 :]
    kept, rest = rest[:INPUTS], rest[INPUTS:]
    fwd_table, xphase, lists, counts, targets, inv_table, local_w, proj, spec_w = kept
    (
    fbuf, pbuf, p_turned, f_share, d_buf, cell_table, rhs, back_part, inv_rows, inv_share, tgt, tgt_send, tgt_share, acc, local_acc,
    ca_send, ca_recv, cb_send, cb_recv, sa_send, sa_recv, sb_send, sb_recv, cg_send, cg_recv,
    ba_send, ba_recv, bb_send, bb_recv, bg_send, bg_recv,
    l_recv, m_send, m_recv, n_send, n_recv,
    load_sem, send_sem, recv_sem, share_send_sem, share_recv_sem,
    ) = rest
    cells = length * length
    width = fields.shape[-1]
    near = slots - 2 * SHARED
    work = slots - SHARED
    units = work * planes
    half = units // 2
    parts = cells // PART
    me = {"fsdp": lax.axis_index("fsdp"), "dp": lax.axis_index("dp")}
    partner = me["dp"] + 1 - 2 * lax.rem(me["dp"], 2)
    offsets = [8 + ((t + 1) // 2) * (1 - 2 * (t % 2)) for t in range(N_DEV - 1)]

    def peer_of(axis, t):
        return lax.rem(me[axis] + offsets[t], N_DEV)

    exchanges = {
        0: ("fsdp", lambda peer: ca_send.at[peer], ca_recv),
        1: ("fsdp", lambda peer: sa_send, sa_recv),
        2: ("dp", lambda peer: cg_send, cg_recv),
        3: ("fsdp", lambda peer: ba_send.at[peer], ba_recv),
        4: ("dp", lambda peer: local_acc.at[peer], l_recv),
        5: ("dp", lambda peer: bg_send, bg_recv),
        6: ("fsdp", lambda peer: m_send, m_recv),
        7: ("dp", lambda peer: n_send, n_recv),
        8: ("fsdp", lambda peer: cb_send.at[peer], cb_recv),
        9: ("fsdp", lambda peer: sb_send, sb_recv),
        10: ("fsdp", lambda peer: bb_send.at[peer], bb_recv),
    }

    def start(phase):
        axis, src, landing = exchanges[phase]
        for t in range(N_DEV - 1):
            peer = peer_of(axis, t)
            pltpu.make_async_remote_copy(
                src_ref=src(peer), dst_ref=landing.at[me[axis]],
                send_sem=send_sem.at[phase], recv_sem=recv_sem.at[phase],
                device_id={axis: peer}, device_id_type=MESH,
            ).start()

    def all_of(phase):
        axis, _, landing = exchanges[phase]
        bytes_of_all = landing.at[pl.ds(0, N_DEV - 1)]
        return pltpu.make_async_remote_copy(
            src_ref=bytes_of_all, dst_ref=bytes_of_all,
            send_sem=send_sem.at[phase], recv_sem=recv_sem.at[phase],
            device_id={axis: peer_of(axis, 0)}, device_id_type=MESH,
        )

    wait_recv = lambda phase: all_of(phase).wait_recv()
    wait_send = lambda phase: all_of(phase).wait_send()

    def share(index, src, dst):
        return pltpu.make_async_remote_copy(
            src_ref=src, dst_ref=dst,
            send_sem=share_send_sem.at[index], recv_sem=share_recv_sem.at[index],
            device_id={"dp": partner}, device_id_type=MESH,
        )

    shares = [
        share(0, tgt_send, tgt_share),
        share(1, pbuf.at[pl.ds(work, SHARED)], f_share),
        share(2, inv_rows.at[pl.ds(units, SHARED * planes)], inv_share),
    ]

    def load(slot):
        return pltpu.make_async_copy(fields.at[slot], fbuf.at[slot], load_sem.at[slot])

    fetches = [
        pltpu.make_async_copy(src, dst, load_sem.at[slots + index]) for index, (src, dst) in enumerate(zip(inputs, kept))
    ]
    for fetch in fetches[:4]:
        fetch.start()
    for slot in range(slots):
        load(slot).start()
    for fetch in fetches[4:]:
        fetch.start()

    barrier = pltpu.get_barrier_semaphore()
    for axis in ("fsdp", "dp"):
        for t in range(N_DEV - 1):
            pl.semaphore_signal(barrier, inc=1, device_id={axis: peer_of(axis, t)}, device_id_type=MESH)

    def x_phase(part_index, k1, plane):
        return xphase[part_index, k1 * length + me["fsdp"] * planes + plane]

    def fold_modes(slot, plane, product):
        direct = product[0:ROWS] + product[ROWS : 2 * ROWS]
        turned = times_i(direct)
        for k1 in range(MX):
            acc[slot, k1] += x_phase(0, k1, plane) * direct - x_phase(1, k1, plane) * turned

    def pack_modes(send, picks):
        for k1 in range(MX):
            for k2 in range(MY):
                send[k1 * MY + k2] = jnp.concatenate([acc[p, k1, 4 * k2 : 4 * k2 + 4] for p in picks], axis=0)

    acc[...] = jnp.zeros_like(acc)
    for fetch in fetches[:4]:
        fetch.wait()
    order = [lists[0, j] for j in range(slots)]
    my_count, partner_count = counts[me["dp"]], counts[partner]
    mine = my_count > 2
    shared_live = jnp.maximum(my_count, partner_count) > 2

    for slot in range(slots):
        load(slot).wait()

        for plane in range(planes):
            fold_modes(slot, plane, dot(fwd_table[...], fbuf[slot, plane]))
    pack_modes(ca_send, order[:near])
    pl.semaphore_wait(barrier, 2 * (N_DEV - 1))
    start(0)
    pack_modes(cb_send, order[near:])

    for fetch in fetches[4:]:
        fetch.wait()
    tgt[...] = jnp.zeros_like(tgt)
    tgt_send[...] = jnp.zeros_like(tgt_send)
    for j in range(SHARED):
        tgt_send[planes * j : planes * (j + 1)] = targets[order[work + j]].astype(jnp.float32)
    shares[0].start()

    def by_position(j):
        def one(plane, carry):
            value = fbuf[order[j], plane]
            pbuf[j, plane] = value
            if j < near:
                p_turned[j, plane] = value.T
            return carry

        lax.fori_loop(0, planes, one, 0)

    for j in range(work, slots):
        by_position(j)
    shares[1].start()
    ca_recv[me["fsdp"]] = ca_send[me["fsdp"]]
    cb_recv[me["fsdp"]] = cb_send[me["fsdp"]]
    start(8)
    for j in range(work):
        tgt[planes * j : planes * (j + 1)] = targets[order[j]].astype(jnp.float32)
        by_position(j)
    grid_total = counts[0]
    for lane in range(1, N_DEV):
        grid_total = grid_total + counts[lane]
    scale = 1.0 / (jnp.zeros((1, width), jnp.float32) + grid_total.astype(jnp.float32))
    root_scale = jnp.sqrt(scale)

    def root_of(unit):
        slot = unit // planes
        live = jnp.where(slot < near, jnp.where(slot < my_count, 1, 0), jnp.where(shared_live, 1, 0))
        return root_scale * live.astype(jnp.float32)

    picks = lax.broadcasted_iota(jnp.int32, (width, width), 0)

    def clear_rhs(unit, carry):
        rhs[unit] = jnp.zeros((2 * width, 2 * width), jnp.bfloat16)
        rhs[unit, 0:width, 0:width] = local_w[...]
        left_over = root_of(unit)
        block = jnp.zeros((width, width), jnp.bfloat16)
        for copy in range(3):
            piece = left_over.astype(jnp.bfloat16).astype(jnp.float32)
            block = block + jnp.where(picks == 3 * ROWS + 16 * copy + unit, piece, 0.0).astype(jnp.bfloat16)
            left_over = left_over - piece
        rhs[unit, width : 2 * width, width : 2 * width] = block
        return carry

    lax.fori_loop(0, units, clear_rhs, 0)
    back_part[...] = jnp.zeros_like(back_part)
    acc[...] = jnp.zeros_like(acc)
    local_acc[...] = jnp.zeros_like(local_acc)
    d_buf[...] = jnp.zeros_like(d_buf)
    shares[0].wait_recv()
    tgt[half : 2 * half] = jnp.where(mine, tgt[half : 2 * half], tgt_share[0:half])
    cell_rows = jnp.concatenate(
        [inv_table[...]] + [tgt[...].astype(jnp.bfloat16)] * 3 + [jnp.zeros((width - 3 * ROWS - 48, cells), jnp.bfloat16)], axis=0
    )
    cell_table[...] = cell_rows.T

    def sum_of(ref):
        value = ref[0]
        for peer in range(1, N_DEV):
            value = value + ref[peer]
        return value

    def mix(landing, send):
        coeff = (sum_of(landing) * float(length) ** -1.5).astype(jnp.bfloat16)
        coeff_f = coeff.astype(jnp.float32)
        turned = times_i(coeff_f).astype(jnp.bfloat16)
        third = (lax.broadcasted_iota(jnp.int32, coeff.shape, 0) // 2) % 2
        mixed = [dot(coeff, spec_w[k3, 0]) + dot(turned, spec_w[k3, 1]) for k3 in range(MZ)]
        send[...] = jnp.where(third == 0, mixed[0], mixed[1]).astype(jnp.bfloat16)
        return coeff_f

    wait_recv(0)
    coeff_near = mix(ca_recv, sa_send)
    start(1)
    wait_recv(8)
    coeff_far = mix(cb_recv, sb_send)
    start(9)
    cg_send[...] = jnp.concatenate([coeff_near, coeff_far], axis=0)
    sa_recv[me["fsdp"]] = sa_send[...]
    sb_recv[me["fsdp"]] = sb_send[...]
    cg_recv[me["dp"]] = cg_send[...]

    def inverse_rows(landing, first, last):
        for k1 in range(MX):
            owners = [landing[k1 * MY + k2].astype(jnp.float32) for k2 in range(MY)]
            for j in range(last - first):
                piece = jnp.concatenate([o[4 * j : 4 * j + 4] for o in owners], axis=0)
                turned_piece = times_i(piece)
                for plane in range(planes):
                    term = x_phase(0, k1, plane) * piece + x_phase(1, k1, plane) * turned_piece
                    unit = (first + j) * planes + plane
                    if k1 == 0:
                        inv_rows[unit] = term
                    else:
                        inv_rows[unit] += term

    start(2)
    shares[1].wait_recv()

    def choose(k, carry):
        slot, plane = near + k // planes, k % planes
        value = jnp.where(mine, pbuf[slot, plane], f_share[k // planes, plane])
        pbuf[slot, plane] = value
        p_turned[slot, plane] = value.T
        return carry

    lax.fori_loop(0, half, choose, 0)
    wait_recv(1)
    inverse_rows(sa_recv, 0, near)

    def set_rhs(first, last):
        for unit in range(first, last):
            values = inv_rows[unit]
            high = values.astype(jnp.bfloat16)
            low = (values - high.astype(jnp.float32)).astype(jnp.bfloat16)
            rhs[unit, width : width + 3 * ROWS, 0:width] = jnp.concatenate([high, high, low], axis=0)

    set_rhs(0, half)

    def reduce_part(unit, part_index):
        slot, plane = unit // planes, unit % planes
        rows_here = pl.ds(part_index * PART, PART)
        left = jnp.concatenate([p_turned[slot, plane, :, rows_here], fwd_table[:, rows_here]], axis=0)
        product = dot(left, d_buf[part_index])
        local_acc[...] += product[0:width, 0:width].reshape(local_acc.shape)
        if part_index == parts - 1:
            fold_modes(slot, plane, back_part[...] + product[width:, 0:width])
        else:
            back_part[...] = product[width:, 0:width]

    def point(unit):
        slot, plane = unit // planes, unit % planes
        root_proj = 0.5 * proj[...] * root_of(unit)
        bell_proj = 2.0 * INV_ROOT_TWO_PI * root_proj
        for part_index in range(parts):
            rows_here = pl.ds(part_index * PART, PART)
            left = jnp.concatenate([pbuf[slot, plane, rows_here], cell_table[rows_here]], axis=1)
            both = dot(left, rhs[unit])
            pre, target = both[:, 0:width], both[:, width : 2 * width]
            gate = lax.erf(pre * ROOT_HALF) + 1.0
            bell = jnp.exp2(pre * pre * (-0.5 * LOG2_E))
            active = gate * root_proj
            pred = jnp.sum(pre * active, axis=1, keepdims=True)
            slope = active + pre * bell * bell_proj
            d_buf[part_index, :, 0:width] = ((pred - target) * slope).astype(jnp.bfloat16)
            if part_index == 0:
                reduce_part(jnp.maximum(unit - 1, 0), parts - 1)
            else:
                reduce_part(unit, part_index - 1)

    def step(index, carry):
        first = index * UNROLL

        @pl.when(first == planes)
        def _():
            wait_recv(9)
            inverse_rows(sb_recv, near, slots)
            shares[2].start()

        @pl.when(first == half)
        def _():
            shares[2].wait_recv()
            inv_rows[half:units] = jnp.where(mine, inv_rows[half:units], inv_share[0:half])
            set_rhs(half, units)

        @pl.when(first == half + planes)
        def _():
            pack_modes(ba_send, range(near))
            start(3)
            ba_recv[me["fsdp"]] = ba_send[me["fsdp"]]

        for sub in range(UNROLL):
            point(first + sub)
        return carry

    lax.fori_loop(0, units // UNROLL, step, 0)
    reduce_part(units - 1, parts - 1)

    start(4)
    pack_modes(bb_send, range(near, work))
    start(10)
    l_recv[me["dp"]] = local_acc[me["dp"]]
    bb_recv[me["fsdp"]] = bb_send[me["fsdp"]]
    back_scale = float(MX * MY * MZ) ** -0.5
    wait_recv(3)
    near_value = sum_of(ba_recv) * back_scale

    wait_recv(4)
    m_value = sum_of(l_recv)
    m_send[...] = m_value
    start(6)
    m_recv[me["fsdp"]] = m_value
    wait_recv(10)
    bg_send[...] = jnp.concatenate([near_value, sum_of(bb_recv) * back_scale], axis=0)
    start(5)
    bg_recv[me["dp"]] = bg_send[...]

    wait_recv(2)
    first, far = 4 * near, 4 * work
    pieces = []
    for lane in range(N_DEV):
        taken = jnp.where(counts[lane] > 2, cg_recv[lane, first:far], cg_recv[lane ^ 1, far : 4 * slots])
        pieces += [cg_recv[lane, 0:first], taken]
    coeff_all = jnp.concatenate(pieces, axis=0)
    every = N_DEV * far
    third = (lax.broadcasted_iota(jnp.int32, (every, width), 0) // 2) % 2
    left = jnp.concatenate([jnp.where(third == k3, coeff_all, 0.0) for k3 in range(MZ)], axis=1)
    left = left.astype(jnp.bfloat16).T

    wait_recv(6)
    n_value = sum_of(m_recv)
    n_send[...] = n_value
    start(7)
    n_recv[me["dp"]] = n_value

    wait_recv(5)
    back_all = bg_recv[...].reshape(every, width)
    right = jnp.concatenate([back_all, -times_i(back_all)], axis=1)
    right_high = right.astype(jnp.bfloat16)
    right_low = (right - right_high.astype(jnp.float32)).astype(jnp.bfloat16)
    grad = dot(left, right_high) + dot(left, right_low)
    for k3 in range(MZ):
        for part_index in range(2):
            out_spec[k3, part_index] = grad[
                k3 * width : (k3 + 1) * width, part_index * width : (part_index + 1) * width
            ]

    wait_recv(7)
    out_local[...] = n_recv[...].reshape(width, width)
    for phase in exchanges:
        wait_send(phase)
    for one in shares:
        one.wait_send()


def copy_out(spec_in, local_in, out_spec, out_local, sem):
    copies = [
        pltpu.make_async_copy(src, dst, sem.at[index])
        for index, (src, dst) in enumerate(((spec_in, out_spec), (local_in, out_local)))
    ]
    for copy in copies:
        copy.start()
    for copy in copies:
        copy.wait()


def body(fields, targets, lists, counts, spectral_w, local_w, proj):
    _, slots, planes, length, _, width = fields.shape
    cells = length * length
    work, near = slots - SHARED, slots - 2 * SHARED
    xphase, fwd_table, inv_table = tables(length)
    vmem = pl.BlockSpec(memory_space=pltpu.VMEM)
    f32, bf16 = jnp.float32, jnp.bfloat16
    results = (
        jax.ShapeDtypeStruct(spectral_w.shape, f32),
        jax.ShapeDtypeStruct(local_w.shape, f32),
    )
    fixed = (
        jnp.asarray(fwd_table), jnp.asarray(xphase), lists, counts, targets.reshape(slots, planes, cells),
        jnp.asarray(inv_table), local_w, proj.reshape(1, width), spectral_w,
    )
    in_smem = (1, 2, 3)
    eight = pltpu.VMEM((N_DEV, 8, width), f32)
    sixteen = pltpu.VMEM((N_DEV, 4 * (slots - near), width), f32)
    hbm = pl.BlockSpec(memory_space=pltpu.HBM)
    grads = pl.pallas_call(
        functools.partial(kernel, length, slots, planes),
        out_shape=tuple(pltpu.VMEM(r.shape, r.dtype) for r in results),
        in_specs=[hbm] * (1 + INPUTS),
        out_specs=(vmem, vmem),
        scratch_shapes=[
            *((pltpu.SMEM if index in in_smem else pltpu.VMEM)(a.shape, a.dtype) for index, a in enumerate(fixed)),
            pltpu.VMEM((slots, planes, cells, width), bf16),
            pltpu.VMEM((slots, planes, cells, width), bf16),
            pltpu.VMEM((work, planes, width, cells), bf16),
            pltpu.VMEM((SHARED, planes, cells, width), bf16),
            pltpu.VMEM((cells // PART, PART, 2 * width), bf16),
            pltpu.VMEM((cells, width), bf16),
            pltpu.VMEM((work * planes, 2 * width, 2 * width), bf16),
            pltpu.VMEM((2 * ROWS, width), f32),
            pltpu.VMEM((slots * planes, ROWS, width), f32),
            pltpu.VMEM((SHARED * planes, ROWS, width), f32),
            pltpu.VMEM((16, cells), f32), pltpu.VMEM((8, cells), f32), pltpu.VMEM((8, cells), f32),
            pltpu.VMEM((slots, MX, ROWS, width), f32),
            pltpu.VMEM((N_DEV, width // N_DEV, width), f32),
            eight, eight, sixteen, sixteen,
            pltpu.VMEM((8, width), bf16), pltpu.VMEM((N_DEV, 8, width), bf16),
            pltpu.VMEM((16, width), bf16), pltpu.VMEM((N_DEV, 16, width), bf16),
            pltpu.VMEM((4 * slots, width), f32), pltpu.VMEM((N_DEV, 4 * slots, width), f32),
            eight, eight, eight, eight,
            pltpu.VMEM((4 * work, width), f32), pltpu.VMEM((N_DEV, 4 * work, width), f32),
            eight,
            pltpu.VMEM((8, width), f32), eight,
            pltpu.VMEM((8, width), f32), eight,
            pltpu.SemaphoreType.DMA((slots + INPUTS,)),
            pltpu.SemaphoreType.DMA((11,)),
            pltpu.SemaphoreType.DMA((11,)),
            pltpu.SemaphoreType.DMA((3,)),
            pltpu.SemaphoreType.DMA((3,)),
        ],
        compiler_params=pltpu.CompilerParams(
            collective_id=0, has_side_effects=True, vmem_limit_bytes=48 * 1024 * 1024,

        ),
        name="fno_step",
    )(*(pltpu.with_memory_space_constraint(a, pltpu.HBM) for a in (fields.reshape(slots, planes, cells, width), *fixed)))
    return pl.pallas_call(
        copy_out, out_shape=results, in_specs=[vmem, vmem], out_specs=(hbm, hbm), name="copy_out",
        scratch_shapes=[pltpu.SemaphoreType.DMA((2,))],
        compiler_params=pltpu.CompilerParams(vmem_limit_bytes=2 * 1024 * 1024),
    )(*grads)


def solution(mesh):
    return jax.shard_map(
        body,
        mesh=mesh,
        in_specs=(
            P("dp", None, "fsdp", None, None, None),
            P("dp", None, "fsdp", None),
            P("dp", None),
            P(),
            P("fsdp", None, None, None),
            P(),
            P(),
        ),
        out_specs=(P("fsdp", None, None, None), P()),
        check_vma=False,
    )
```
